32 devices in a mesh: bin: 4 (over x, core), slab: 8 (over z, y).
Axes of the slice: x: 2, y: 2, z: 4, core: 2. Of those that a mesh axis runs over, the one named last changes fastest.
Arguments:
- volumes: float32 [8, 32, 64, 512], P('bin', 'slab'), may hold values from -6 to 6
- attenuation: float32 [8, 3], replicated, may hold values from 0.2 to 1.2
- penalty: float32 [1], replicated, may hold values from 0.2 to 0.4
- tv_weight: float32 [1], replicated, may hold values from 0.3 to 0.8
Outputs:
- materials: float32 [3, 32, 64, 512], P(None, ('bin', 'slab'))
The draws below stay inside these ranges and needn't reach their ends.
All inputs are finite; a program needn't handle non-finite values.
Results may differ from the reference program's by a relative error of at most 0.0001.
Values sent between devices are 32-bit elements; how exact they have to be, the bound alone decides.
No kernel may reach another device: no remote copies, remote signals or barrier semaphores. Data moves between devices by JAX's collectives and lax.ppermute only.
A program may use at most 64 MiB of HBM per device.

```python
import math
import jax
import jax.numpy as jnp
from jax import lax

BINS = 8
MATS = 3
NX = 512
ITERS = 3
NZ = 32
NY = 64


def block_levels(rng, shape, shards, least, largest):
    factor_of = 1.0
    for position, blocks in shards:
        heights = jax.random.uniform(jax.random.fold_in(jax.random.fold_in(rng, 6), position), (blocks,), jnp.float32, least / len(shards), largest / len(shards))
        factor_of = factor_of * jnp.repeat(jnp.exp(heights), shape[position] // blocks).reshape((-1,) + (1,) * (len(shape) - 1 - position))
    return factor_of


def bell_draw(own_key, shape, width, bound, cuts=(), kind=jnp.bfloat16):
    drawn = width * jax.random.normal(own_key, shape, jnp.float32)
    if cuts:
        drawn = drawn * block_levels(own_key, shape, cuts, -0.22, 0.18)
    return jnp.clip(drawn, -bound, bound).astype(kind)


def setup_inputs(seed: int = 0) -> dict:
    key_list = jax.random.split(jax.random.key(seed), 5)
    return {
        "volumes": bell_draw(key_list[0], (BINS, NZ, NY, NX), 1.0, 6.0, ((0, 4), (1, 8)), jnp.float32),
        "attenuation": jnp.clip(jax.random.uniform(key_list[1], (BINS, MATS), jnp.float32, 0.2, 1.2), 0.2, 1.2),
        "penalty": jnp.clip(jnp.exp(jax.random.uniform(key_list[2], (1,), jnp.float32, math.log(0.2), math.log(0.4))), 0.2, 0.4),
        "tv_weight": jnp.clip(jnp.exp(jax.random.uniform(key_list[3], (1,), jnp.float32, math.log(0.3), math.log(0.8))), 0.3, 0.8),
    }


def inverse_three(matrix):
    cofactor = [[matrix[(row + 1) % 3, (col + 1) % 3] * matrix[(row + 2) % 3, (col + 2) % 3] - matrix[(row + 1) % 3, (col + 2) % 3] * matrix[(row + 2) % 3, (col + 1) % 3] for col in range(3)] for row in range(3)]
    determinant = matrix[0, 0] * cofactor[0][0] + matrix[0, 1] * cofactor[0][1] + matrix[0, 2] * cofactor[0][2]
    return [[cofactor[col][row] / determinant for col in range(3)] for row in range(3)]

def normal_inverse(attenuation, penalty_value):
    gram = jnp.dot(attenuation.T, attenuation, precision=lax.Precision.HIGHEST)
    gram = gram + 12.0 * penalty_value * jnp.eye(3, dtype=jnp.float32)
    return inverse_three(gram)

def apply_inverse(inverse, fields):
    return jnp.stack([inverse[row][0] * fields[0] + inverse[row][1] * fields[1] + inverse[row][2] * fields[2] for row in range(3)])

def project(attenuation, volumes):
    return jnp.einsum('km,kzyx->mzyx', attenuation, volumes, precision=lax.Precision.HIGHEST)

def forward_diff(field, axis):
    count = field.shape[axis]
    upper = lax.slice_in_dim(field, 1, count, axis=axis)
    lower = lax.slice_in_dim(field, 0, count - 1, axis=axis)
    zeros = jnp.zeros_like(lax.slice_in_dim(field, 0, 1, axis=axis))
    return jnp.concatenate([upper - lower, zeros], axis)

def gradient(field):
    return [forward_diff(field, 1), forward_diff(field, 2), forward_diff(field, 3)]

def divergence(parts):
    total = jnp.zeros_like(parts[0])
    for axis, part in zip((1, 2, 3), parts):
        count = part.shape[axis]
        earlier = jnp.concatenate([jnp.zeros_like(lax.slice_in_dim(part, 0, 1, axis=axis)), lax.slice_in_dim(part, 0, count - 1, axis=axis)], axis)
        total = total + (part - earlier)
    return total

def clip_group(parts, threshold):
    squares = lax.optimization_barrier(jnp.sum(parts[0] * parts[0], axis=0)) + lax.optimization_barrier(jnp.sum(parts[1] * parts[1], axis=0)) + lax.optimization_barrier(jnp.sum(parts[2] * parts[2], axis=0))
    scale = threshold / jnp.maximum(jnp.sqrt(squares), threshold)
    return [part * scale[None] for part in parts]

def reference(volumes, attenuation, penalty, tv_weight):
    penalty_value = penalty[0]
    threshold = tv_weight[0] / penalty_value
    inverse = normal_inverse(attenuation, penalty_value)
    data = project(attenuation, volumes)
    field = apply_inverse(inverse, data)
    dual = clip_group(gradient(field), threshold)
    step_parts = [2.0 * part for part in dual]
    for turn in range(ITERS):
        field = apply_inverse(inverse, data + 12.0 * penalty_value * field + penalty_value * divergence(step_parts))
        if turn < ITERS - 1:
            grads = gradient(field)
            fresh = clip_group([grads[index] + dual[index] for index in range(3)], threshold)
            step_parts = [2.0 * fresh[index] - dual[index] for index in range(3)]
            dual = fresh
    return field
```

```python
import functools

import jax
import jax.numpy as jnp
from jax import lax
from jax.experimental import pallas as pl
from jax.experimental.pallas import tpu as pltpu
from jax.sharding import PartitionSpec as P

ITERS = 3
EDGE = 4
VMEM = pltpu.VMEM
SMEM = pltpu.SMEM


def window_start(quarter, rows, total):
    return min(max(rows * quarter - EDGE, 0), total - rows - 2 * EDGE)


def inverse_three(m):
    cof = [
        [
            m[(r + 1) % 3][(c + 1) % 3] * m[(r + 2) % 3][(c + 2) % 3]
            - m[(r + 1) % 3][(c + 2) % 3] * m[(r + 2) % 3][(c + 1) % 3]
            for c in range(3)
        ]
        for r in range(3)
    ]
    det = m[0][0] * cof[0][0] + m[0][1] * cof[0][1] + m[0][2] * cof[0][2]
    return [[cof[c][r] / det for c in range(3)] for r in range(3)]


def normal_inverse(att, pen, bins):
    gram = [[None] * 3 for _ in range(3)]
    for i in range(3):
        for j in range(i, 3):
            total = att[0, i] * att[0, j]
            for k in range(1, bins):
                total = total + att[k, i] * att[k, j]
            gram[i][j] = gram[j][i] = total
    for i in range(3):
        gram[i][i] = gram[i][i] + 12.0 * pen
    return inverse_three(gram)


def project_kernel(dims, att, pen, mine, other, own, to_x, to_y, to_xy, part):
    bins, rows, total, lanes = dims
    b = lax.axis_index("bin")
    s = lax.axis_index("slab")
    inv = normal_inverse(att, pen[0], bins)

    def weights(first):
        out = []
        for k in range(2):
            a = [att[first + k, m] for m in range(3)]
            out.append([inv[m][0] * a[0] + inv[m][1] * a[1] + inv[m][2] * a[2] for m in range(3)])
        return out

    w = weights(2 * b) + weights(2 * (b ^ 1))
    for layer in range(2):

        def body(t, carry, layer=layer):
            at = pl.ds(pl.multiple_of(t * 8, 8), 8)
            v = [mine[0, layer, at, :], mine[1, layer, at, :], other[0, layer, at, :], other[1, layer, at, :]]
            for m in range(3):
                part[m, layer, at, :] = v[0] * w[0][m] + v[1] * w[1][m] + (v[2] * w[2][m] + v[3] * w[3][m])
            return carry

        lax.fori_loop(0, total // 8, body, 0)
    me = 2 * (b // 2) + s % 2
    width = rows + 2 * EDGE
    for rel, ref in enumerate((own, to_y, to_x, to_xy)):
        for quarter in range(4):

            @pl.when((me ^ rel) == quarter)
            def _(ref=ref, quarter=quarter):
                start = window_start(quarter, rows, total)
                ref[...] = part[:, :, start : start + width, :]


def sum_kernel(own, from_x, from_y, from_xy, pair, far, near, cross):
    y = lax.axis_index("slab") % 2
    c = lax.axis_index("bin") % 2
    for m in range(3):
        for layer in range(2):
            a = own[m, layer] + from_x[m, layer]
            d = from_y[m, layer] + from_xy[m, layer]
            pair[y, m, layer] = a
            pair[1 - y, m, layer] = d
    far[...] = pair[c]
    for m in range(3):
        near[m, 0] = pair[1 - c, m, 1 - c]

        @pl.when(c == 0)
        def _(m=m):
            cross[m, 0] = pair[0, m, 1]
            cross[m, 1] = pair[1, m, 0]
            cross[m, 2] = pair[1, m, 1]

        @pl.when(c == 1)
        def _(m=m):
            cross[m, 0] = pair[0, m, 0]
            cross[m, 1] = pair[0, m, 1]
            cross[m, 2] = pair[1, m, 0]


def iterate_kernel(dims, att, pen, tvw, pair, far, near, cross, *refs):
    bins, rows, total, lanes, depth = dims
    outs, (first, field, dual, down) = refs[:4], refs[4:]
    width = rows + 2 * EDGE
    tiles, columns = width // 8, lanes // 128
    b = lax.axis_index("bin")
    s = lax.axis_index("slab")
    c = b % 2
    me = 2 * (b // 2) + s % 2
    z_base = (s // 2) * 8 + 4 * c - 3
    pen_value = pen[0]
    inv = normal_inverse(att, pen_value, bins)
    inv = [[pen_value * e for e in row] for row in inv]
    threshold = tvw[0] / pen_value
    squared = threshold * threshold

    def put(index, source):
        first[:, index] = source

    @pl.when(c == 0)
    def _():
        put(0, near[:, 0])
        put(1, far[:, 0])
        put(2, far[:, 1])
        put(3, pair[0, :, 0])
        put(4, pair[0, :, 1])
        put(5, cross[:, 0])
        put(6, cross[:, 1])
        put(7, pair[1, :, 0])
        put(8, pair[1, :, 1])
        put(9, cross[:, 2])

    @pl.when(c == 1)
    def _():
        put(0, cross[:, 0])
        put(1, pair[0, :, 0])
        put(2, pair[0, :, 1])
        put(3, cross[:, 1])
        put(4, cross[:, 2])
        put(5, pair[1, :, 0])
        put(6, pair[1, :, 1])
        put(7, far[:, 0])
        put(8, far[:, 1])
        put(9, near[:, 0])

    lane = lax.broadcasted_iota(jnp.int32, (8, 128), 1)
    sub = lax.broadcasted_iota(jnp.int32, (8, 128), 0)
    last_lane, first_lane = lane == 127, lane == 0
    last_sub, first_sub = sub == 7, sub == 0
    at_end = last_sub & (me == 3)
    zero = jnp.zeros((8, 128), jnp.float32)

    for turn in range(ITERS):
        src = first if turn == 0 else field
        final = turn == ITERS - 1

        def layer_step(i, lead, src=src, turn=turn, final=final):
            z = z_base + i
            z_inside = ((z >= 0) & (z < depth - 1)).astype(jnp.float32)

            def load(ref, m, layer, t, col):
                return ref[m, layer, 8 * t : 8 * t + 8, 128 * col : 128 * col + 128]

            right = [None] * tiles
            for col in range(columns):
                below = None
                f = [load(src, m, i, 0, col) for m in range(3)]
                for t in range(tiles):
                    following = None
                    if t + 1 < tiles:
                        following = [load(src, m, i, t + 1, col) for m in range(3)]
                    v = []
                    for m in range(3):
                        gz = (load(src, m, i + 1, t, col) - f[m]) * z_inside
                        up = pltpu.roll(f[m], 7, 0)
                        if following is not None:
                            up = jnp.where(last_sub, pltpu.roll(following[m], 7, 0), up)
                        else:
                            up = jnp.where(at_end, f[m], up)
                        nxt = f[m]
                        if col + 1 < columns:
                            nxt = pltpu.roll(load(src, m, i, t, col + 1), 127, 1)
                        ahead = jnp.where(last_lane, nxt, pltpu.roll(f[m], 127, 1))
                        v.append([gz, up - f[m], ahead - f[m]])
                    old = None
                    if turn > 0:
                        old = [[load(dual, 3 * m + d, i, t, col) for d in range(3)] for m in range(3)]
                        v = [[v[m][d] + old[m][d] for d in range(3)] for m in range(3)]
                    squares = [v[m][0] * v[m][0] + v[m][1] * v[m][1] + v[m][2] * v[m][2] for m in range(3)]
                    scale = threshold * lax.rsqrt(jnp.maximum(squares[0] + squares[1] + squares[2], squared))
                    fresh = [[v[m][d] * scale for d in range(3)] for m in range(3)]
                    if not final:
                        for m in range(3):
                            for d in range(3):
                                dual[3 * m + d, i, 8 * t : 8 * t + 8, 128 * col : 128 * col + 128] = fresh[m][d]
                    step = [[fresh[m][d] + fresh[m][d] for d in range(3)] for m in range(3)]
                    if turn > 0:
                        step = [[step[m][d] - old[m][d] for d in range(3)] for m in range(3)]
                    lower = None
                    if not lead:
                        lower = [down[m, 8 * t : 8 * t + 8, 128 * col : 128 * col + 128] for m in range(3)]
                    for m in range(3):
                        down[m, 8 * t : 8 * t + 8, 128 * col : 128 * col + 128] = step[m][0]
                    if not lead:
                        rolled_y = [pltpu.roll(step[m][1], 1, 0) for m in range(3)]
                        rolled_x = [pltpu.roll(step[m][2], 1, 1) for m in range(3)]
                        rhs = []
                        for m in range(3):
                            prev_y = jnp.where(first_sub, zero if below is None else below[m], rolled_y[m])
                            prev_x = jnp.where(first_lane, zero if right[t] is None else right[t][m], rolled_x[m])
                            div = (step[m][0] - lower[m]) + (step[m][1] - prev_y) + (step[m][2] - prev_x)
                            rhs.append(12.0 * f[m] + div)
                        below, right[t] = rolled_y, rolled_x
                        for m in range(3):
                            field[m, i, 8 * t : 8 * t + 8, 128 * col : 128 * col + 128] = (
                                load(first, m, i, t, col)
                                + (inv[m][0] * rhs[0] + inv[m][1] * rhs[1] + inv[m][2] * rhs[2])
                            )
                    f = following

        layer_step(turn, True)

        def body(i, carry, layer_step=layer_step):
            layer_step(i, False)
            return carry

        lax.fori_loop(turn + 1, 9 - turn, body, 0)

    for quarter in range(4):

        @pl.when(me == quarter)
        def _(quarter=quarter):
            at = rows * quarter - window_start(quarter, rows, total)
            for j in range(4):
                outs[j ^ quarter][...] = field[:, 3 + j, at : at + rows, :]


def gather_kernel(rows, r0, r1, r2, r3, out):
    j = lax.axis_index("slab") % 4
    for t, ref in enumerate((r0, r1, r2, r3)):
        at = pl.multiple_of((j ^ t) * rows, 8)
        out[:, 0, pl.ds(at, rows), :] = ref[...]


def call(kernel, outs, args, smem=0, scratch=()):
    shapes = [jax.ShapeDtypeStruct(o, jnp.float32) for o in outs]
    return pl.pallas_call(
        kernel,
        out_shape=shapes,
        in_specs=[pl.BlockSpec(memory_space=SMEM)] * smem
        + [pl.BlockSpec(memory_space=VMEM)] * (len(args) - smem),
        out_specs=[pl.BlockSpec(memory_space=VMEM)] * len(outs),
        scratch_shapes=list(scratch),
    )(*args)


def on_device(mesh_bin, mesh_slab, volumes, attenuation, penalty, tv_weight):
    own_bins, layers, total, lanes = volumes.shape
    bins = own_bins * mesh_bin
    assert mesh_bin == 4 and own_bins == 2 and layers == 4 and mesh_slab % 4 == 0
    rows = total // 4
    width = rows + 2 * EDGE
    depth = layers * mesh_slab
    devices = [(b, s) for b in range(mesh_bin) for s in range(mesh_slab)]

    def send(x, where):
        pairs = []
        for b, s in devices:
            to = where(b, s)
            if 0 <= to[0] < mesh_bin and 0 <= to[1] < mesh_slab:
                pairs.append((b * mesh_slab + s, to[0] * mesh_slab + to[1]))
        return lax.ppermute(x, ("bin", "slab"), pairs)

    c = lax.axis_index("bin") % 2
    away = lax.dynamic_slice_in_dim(volumes, 2 * (1 - c), 2, 1)
    mine = lax.dynamic_slice_in_dim(volumes, 2 * c, 2, 1)
    other = send(away, lambda b, s: (b ^ 1, s))

    win = (3, 2, width, lanes)
    own, to_x, to_y, to_xy = call(
        functools.partial(project_kernel, (bins, rows, total, lanes)),
        [win] * 4,
        (attenuation, penalty, mine, other),
        smem=2,
        scratch=[VMEM((3, 2, total, lanes), jnp.float32)],
    )
    from_xy = send(to_xy, lambda b, s: (b ^ 2, s ^ 1))
    from_x = send(to_x, lambda b, s: (b ^ 2, s))
    from_y = send(to_y, lambda b, s: (b, s ^ 1))
    pair, far, near, cross = call(
        sum_kernel,
        [(2,) + win, win, (3, 1, width, lanes), (3, 3, width, lanes)],
        (own, from_x, from_y, from_xy),
    )
    far = send(far, lambda b, s: (b ^ 1, s + (2 if b % 2 else -2)))
    near = send(near, lambda b, s: (b, s + (-2 if b % 2 else 2)))
    cross = send(cross, lambda b, s: (b ^ 1, s))
    blocks = call(
        functools.partial(iterate_kernel, (bins, rows, total, lanes, depth)),
        [(3, rows, lanes)] * 4,
        (attenuation, penalty, tv_weight, pair, far, near, cross),
        smem=3,
        scratch=[
            VMEM((3, 10, width, lanes), jnp.float32),
            VMEM((3, 10, width, lanes), jnp.float32),
            VMEM((9, 9, width, lanes), jnp.float32),
            VMEM((3, width, lanes), jnp.float32),
        ],
    )

    def owner(t):
        def where(b, s):
            j = t ^ (2 * (b // 2) + s % 2)
            z = (s // 2) * 8 + 4 * (b % 2) + j
            return z // mesh_slab, z % mesh_slab

        return where

    blocks = [send(block, owner(t)) for t, block in enumerate(blocks)]
    return call(functools.partial(gather_kernel, rows), [(3, 1, total, lanes)], blocks)[0]


def solution(mesh):
    placed = (P("bin", "slab", None, None), P(), P(), P())
    return jax.shard_map(
        functools.partial(on_device, mesh.shape["bin"], mesh.shape["slab"]),
        mesh=mesh,
        in_specs=placed,
        out_specs=P(None, ("bin", "slab"), None, None),
        check_vma=False,
    )
```

```python
import functools
import math

import jax
import jax.numpy as jnp
from jax import lax
from jax.experimental import pallas as pl
from jax.experimental.pallas import tpu as pltpu
from jax.sharding import PartitionSpec as P

ITERS = 3
EDGE = 4
VMEM = pltpu.VMEM
SMEM = pltpu.SMEM


def window_start(quarter, rows, total):
    return min(max(rows * quarter - EDGE, 0), total - rows - 2 * EDGE)


def inverse_three(m):
    cof = [
        [
            m[(r + 1) % 3][(c + 1) % 3] * m[(r + 2) % 3][(c + 2) % 3]
            - m[(r + 1) % 3][(c + 2) % 3] * m[(r + 2) % 3][(c + 1) % 3]
            for c in range(3)
        ]
        for r in range(3)
    ]
    det = m[0][0] * cof[0][0] + m[0][1] * cof[0][1] + m[0][2] * cof[0][2]
    return [[cof[c][r] / det for c in range(3)] for r in range(3)]


def normal_inverse(att, pen, bins):
    gram = [[None] * 3 for _ in range(3)]
    for i in range(3):
        for j in range(i, 3):
            total = att[i, 0] * att[j, 0]
            for k in range(1, bins):
                total = total + att[i, k] * att[j, k]
            gram[i][j] = gram[j][i] = total
    for i in range(3):
        gram[i][i] = gram[i][i] + 12.0 * pen
    return inverse_three(gram)


def project_kernel(dims, att, pen, mine, other, own, to_x, to_y, to_xy, part):
    bins, rows, total, lanes = dims
    b = lax.axis_index("bin")
    s = lax.axis_index("slab")
    inv = normal_inverse(att, pen[0], bins)

    def weights(first):
        out = []
        for k in range(2):
            a = [att[m, first + k] for m in range(3)]
            out.append([inv[m][0] * a[0] + inv[m][1] * a[1] + inv[m][2] * a[2] for m in range(3)])
        return out

    w = weights(2 * b) + weights(2 * (b ^ 1))
    for layer in range(2):

        def body(t, carry, layer=layer):
            at = pl.ds(pl.multiple_of(t * 8, 8), 8)
            v = [mine[0, layer, at, :], mine[1, layer, at, :], other[0, layer, at, :], other[1, layer, at, :]]
            for m in range(3):
                part[m, layer, at, :] = v[0] * w[0][m] + v[1] * w[1][m] + (v[2] * w[2][m] + v[3] * w[3][m])
            return carry

        lax.fori_loop(0, total // 8, body, 0)
    me = 2 * (b // 2) + s % 2
    width = rows + 2 * EDGE
    for rel, ref in enumerate((own, to_y, to_x, to_xy)):
        for quarter in range(4):

            @pl.when((me ^ rel) == quarter)
            def _(ref=ref, quarter=quarter):
                start = window_start(quarter, rows, total)
                ref[...] = part[:, :, start : start + width, :]


def sum_kernel(own, from_x, from_y, from_xy, pair, far, near, cross):
    y = lax.axis_index("slab") % 2
    c = lax.axis_index("bin") % 2
    for m in range(3):
        for layer in range(2):
            a = own[m, layer] + from_x[m, layer]
            d = from_y[m, layer] + from_xy[m, layer]
            pair[y, m, layer] = a
            pair[1 - y, m, layer] = d
    far[...] = pair[c]
    for m in range(3):
        near[m, 0] = pair[1 - c, m, 1 - c]

        @pl.when(c == 0)
        def _(m=m):
            cross[m, 0] = pair[0, m, 1]
            cross[m, 1] = pair[1, m, 0]
            cross[m, 2] = pair[1, m, 1]

        @pl.when(c == 1)
        def _(m=m):
            cross[m, 0] = pair[0, m, 0]
            cross[m, 1] = pair[0, m, 1]
            cross[m, 2] = pair[1, m, 0]


def iterate_kernel(dims, att, pen, tvw, pair, far, near, cross, *refs):
    bins, rows, total, lanes, depth = dims
    outs, (first, field, dual, down) = refs[:4], refs[4:]
    width = rows + 2 * EDGE
    tiles, columns = width // 8, lanes // 128
    b = lax.axis_index("bin")
    s = lax.axis_index("slab")
    c = b % 2
    me = 2 * (b // 2) + s % 2
    z_base = (s // 2) * 8 + 4 * c - 3
    pen_value = pen[0]
    inv = normal_inverse(att, pen_value, bins)
    inv = [[pen_value * e for e in row] for row in inv]
    threshold = tvw[0] / pen_value
    squared = threshold * threshold

    def put(index, source):
        first[:, index] = source

    @pl.when(c == 0)
    def _():
        put(0, near[:, 0])
        put(1, far[:, 0])
        put(2, far[:, 1])
        put(3, pair[0, :, 0])
        put(4, pair[0, :, 1])
        put(5, cross[:, 0])
        put(6, cross[:, 1])
        put(7, pair[1, :, 0])
        put(8, pair[1, :, 1])
        put(9, cross[:, 2])

    @pl.when(c == 1)
    def _():
        put(0, cross[:, 0])
        put(1, pair[0, :, 0])
        put(2, pair[0, :, 1])
        put(3, cross[:, 1])
        put(4, cross[:, 2])
        put(5, pair[1, :, 0])
        put(6, pair[1, :, 1])
        put(7, far[:, 0])
        put(8, far[:, 1])
        put(9, near[:, 0])

    lane = lax.broadcasted_iota(jnp.int32, (8, 128), 1)
    sub = lax.broadcasted_iota(jnp.int32, (8, 128), 0)
    last_lane, first_lane = lane == 127, lane == 0
    last_sub, first_sub = sub == 7, sub == 0
    at_end = last_sub & (me == 3)
    zero = jnp.zeros((8, 128), jnp.float32)

    for turn in range(ITERS):
        src = first if turn == 0 else field
        final = turn == ITERS - 1

        def layer_step(i, lead, src=src, turn=turn, final=final):
            z = z_base + i
            z_inside = ((z >= 0) & (z < depth - 1)).astype(jnp.float32)

            def load(ref, m, layer, t, col):
                return ref[m, layer, 8 * t : 8 * t + 8, 128 * col : 128 * col + 128]

            right = [None] * tiles
            for col in range(columns):
                below = None
                f = [load(src, m, i, 0, col) for m in range(3)]
                for t in range(tiles):
                    following = None
                    if t + 1 < tiles:
                        following = [load(src, m, i, t + 1, col) for m in range(3)]
                    v = []
                    for m in range(3):
                        gz = (load(src, m, i + 1, t, col) - f[m]) * z_inside
                        up = pltpu.roll(f[m], 7, 0)
                        if following is not None:
                            up = jnp.where(last_sub, pltpu.roll(following[m], 7, 0), up)
                        else:
                            up = jnp.where(at_end, f[m], up)
                        nxt = f[m]
                        if col + 1 < columns:
                            nxt = pltpu.roll(load(src, m, i, t, col + 1), 127, 1)
                        ahead = jnp.where(last_lane, nxt, pltpu.roll(f[m], 127, 1))
                        v.append([gz, up - f[m], ahead - f[m]])
                    old = None
                    if turn > 0:
                        old = [[load(dual, 3 * m + d, i, t, col) for d in range(3)] for m in range(3)]
                        v = [[v[m][d] + old[m][d] for d in range(3)] for m in range(3)]
                    squares = [v[m][0] * v[m][0] + v[m][1] * v[m][1] + v[m][2] * v[m][2] for m in range(3)]
                    scale = threshold * lax.rsqrt(jnp.maximum(squares[0] + squares[1] + squares[2], squared))
                    fresh = [[v[m][d] * scale for d in range(3)] for m in range(3)]
                    if not final:
                        for m in range(3):
                            for d in range(3):
                                dual[3 * m + d, i, 8 * t : 8 * t + 8, 128 * col : 128 * col + 128] = fresh[m][d]
                    step = [[fresh[m][d] + fresh[m][d] for d in range(3)] for m in range(3)]
                    if turn > 0:
                        step = [[step[m][d] - old[m][d] for d in range(3)] for m in range(3)]
                    lower = None
                    if not lead:
                        lower = [down[m, 8 * t : 8 * t + 8, 128 * col : 128 * col + 128] for m in range(3)]
                    for m in range(3):
                        down[m, 8 * t : 8 * t + 8, 128 * col : 128 * col + 128] = step[m][0]
                    if not lead:
                        rolled_y = [pltpu.roll(step[m][1], 1, 0) for m in range(3)]
                        rolled_x = [pltpu.roll(step[m][2], 1, 1) for m in range(3)]
                        rhs = []
                        for m in range(3):
                            prev_y = jnp.where(first_sub, zero if below is None else below[m], rolled_y[m])
                            prev_x = jnp.where(first_lane, zero if right[t] is None else right[t][m], rolled_x[m])
                            div = (step[m][0] - lower[m]) + (step[m][1] - prev_y) + (step[m][2] - prev_x)
                            rhs.append(12.0 * f[m] + div)
                        below, right[t] = rolled_y, rolled_x
                        for m in range(3):
                            field[m, i, 8 * t : 8 * t + 8, 128 * col : 128 * col + 128] = (
                                load(first, m, i, t, col)
                                + (inv[m][0] * rhs[0] + inv[m][1] * rhs[1] + inv[m][2] * rhs[2])
                            )
                    f = following

        layer_step(turn, True)

        def body(i, carry, layer_step=layer_step):
            layer_step(i, False)
            return carry

        lax.fori_loop(turn + 1, 9 - turn, body, 0)

    for quarter in range(4):

        @pl.when(me == quarter)
        def _(quarter=quarter):
            at = rows * quarter - window_start(quarter, rows, total)
            for j in range(4):
                outs[j ^ quarter][...] = field[:, 3 + j, at : at + rows, :]


def gather_kernel(rows, r0, r1, r2, r3, out):
    j = lax.axis_index("slab") % 4
    for t, ref in enumerate((r0, r1, r2, r3)):
        at = pl.multiple_of((j ^ t) * rows, 8)
        out[:, 0, pl.ds(at, rows), :] = ref[...]


def call(kernel, outs, args, smem=0, scratch=()):
    shapes = [jax.ShapeDtypeStruct(o, jnp.float32) for o in outs]
    held = sum(math.prod(a.shape) for a in (*shapes, *args[smem:], *scratch))
    return pl.pallas_call(
        kernel,
        out_shape=shapes,
        in_specs=[pl.BlockSpec(memory_space=SMEM)] * smem
        + [pl.BlockSpec(memory_space=VMEM)] * (len(args) - smem),
        out_specs=[pl.BlockSpec(memory_space=VMEM)] * len(outs),
        scratch_shapes=list(scratch),
        compiler_params=pltpu.CompilerParams(vmem_limit_bytes=4 * held + (2 << 20)),
    )(*args)


def on_device(mesh_bin, mesh_slab, volumes, attenuation, penalty, tv_weight):
    own_bins, layers, total, lanes = volumes.shape
    bins = own_bins * mesh_bin
    assert mesh_bin == 4 and own_bins == 2 and layers == 4 and mesh_slab % 4 == 0
    rows = total // 4
    width = rows + 2 * EDGE
    depth = layers * mesh_slab
    devices = [(b, s) for b in range(mesh_bin) for s in range(mesh_slab)]

    def send(x, where):
        pairs = []
        for b, s in devices:
            to = where(b, s)
            if 0 <= to[0] < mesh_bin and 0 <= to[1] < mesh_slab:
                pairs.append((b * mesh_slab + s, to[0] * mesh_slab + to[1]))
        return lax.ppermute(x, ("bin", "slab"), pairs)

    c = lax.axis_index("bin") % 2
    away = lax.dynamic_slice_in_dim(volumes, 2 * (1 - c), 2, 1)
    mine = lax.dynamic_slice_in_dim(volumes, 2 * c, 2, 1)
    other = send(away, lambda b, s: (b ^ 1, s))

    win = (3, 2, width, lanes)
    own, to_x, to_y, to_xy = call(
        functools.partial(project_kernel, (bins, rows, total, lanes)),
        [win] * 4,
        (attenuation.T, penalty, mine, other),
        smem=2,
        scratch=[VMEM((3, 2, total, lanes), jnp.float32)],
    )
    from_xy = send(to_xy, lambda b, s: (b ^ 2, s ^ 1))
    from_x = send(to_x, lambda b, s: (b ^ 2, s))
    from_y = send(to_y, lambda b, s: (b, s ^ 1))
    pair, far, near, cross = call(
        sum_kernel,
        [(2,) + win, win, (3, 1, width, lanes), (3, 3, width, lanes)],
        (own, from_x, from_y, from_xy),
    )
    far = send(far, lambda b, s: (b ^ 1, s + (2 if b % 2 else -2)))
    near = send(near, lambda b, s: (b, s + (-2 if b % 2 else 2)))
    cross = send(cross, lambda b, s: (b ^ 1, s))
    blocks = call(
        functools.partial(iterate_kernel, (bins, rows, total, lanes, depth)),
        [(3, rows, lanes)] * 4,
        (attenuation.T, penalty, tv_weight, pair, far, near, cross),
        smem=3,
        scratch=[
            VMEM((3, 10, width, lanes), jnp.float32),
            VMEM((3, 10, width, lanes), jnp.float32),
            VMEM((9, 9, width, lanes), jnp.float32),
            VMEM((3, width, lanes), jnp.float32),
        ],
    )

    def owner(t):
        def where(b, s):
            j = t ^ (2 * (b // 2) + s % 2)
            z = (s // 2) * 8 + 4 * (b % 2) + j
            return z // mesh_slab, z % mesh_slab

        return where

    blocks = [send(block, owner(t)) for t, block in enumerate(blocks)]
    return call(functools.partial(gather_kernel, rows), [(3, 1, total, lanes)], blocks)[0]


def solution(mesh):
    placed = (P("bin", "slab", None, None), P(), P(), P())
    return jax.shard_map(
        functools.partial(on_device, mesh.shape["bin"], mesh.shape["slab"]),
        mesh=mesh,
        in_specs=placed,
        out_specs=P(None, ("bin", "slab"), None, None),
        check_vma=False,
    )
```

```python
import functools
import math

import jax
import jax.numpy as jnp
from jax import lax
from jax.experimental import pallas as pl
from jax.experimental.pallas import tpu as pltpu
from jax.sharding import PartitionSpec as P

ITERS = 3
EDGE = 4
VMEM = pltpu.VMEM
SMEM = pltpu.SMEM


def window_start(quarter, rows, total):
    return min(max(rows * quarter - EDGE, 0), total - rows - 2 * EDGE)


def inverse_three(m):
    cof = [
        [
            m[(r + 1) % 3][(c + 1) % 3] * m[(r + 2) % 3][(c + 2) % 3]
            - m[(r + 1) % 3][(c + 2) % 3] * m[(r + 2) % 3][(c + 1) % 3]
            for c in range(3)
        ]
        for r in range(3)
    ]
    det = m[0][0] * cof[0][0] + m[0][1] * cof[0][1] + m[0][2] * cof[0][2]
    return [[cof[c][r] / det for c in range(3)] for r in range(3)]


def normal_inverse(att, pen, bins):
    gram = [[None] * 3 for _ in range(3)]
    for i in range(3):
        for j in range(i, 3):
            total = att[i, 0] * att[j, 0]
            for k in range(1, bins):
                total = total + att[i, k] * att[j, k]
            gram[i][j] = gram[j][i] = total
    for i in range(3):
        gram[i][i] = gram[i][i] + 12.0 * pen
    return inverse_three(gram)


def project_kernel(dims, att, pen, mine, other, own, to_x, to_y, to_xy, part):
    bins, rows, total, lanes = dims
    b = lax.axis_index("bin")
    s = lax.axis_index("slab")
    inv = normal_inverse(att, pen[0], bins)

    def weights(first):
        out = []
        for k in range(2):
            a = [att[m, first + k] for m in range(3)]
            out.append([inv[m][0] * a[0] + inv[m][1] * a[1] + inv[m][2] * a[2] for m in range(3)])
        return out

    w = weights(2 * b) + weights(2 * (b ^ 1))
    for layer in range(2):

        def body(t, carry, layer=layer):
            at = pl.ds(pl.multiple_of(t * 8, 8), 8)
            v = [mine[0, layer, at, :], mine[1, layer, at, :], other[0, layer, at, :], other[1, layer, at, :]]
            for m in range(3):
                part[m, layer, at, :] = v[0] * w[0][m] + v[1] * w[1][m] + (v[2] * w[2][m] + v[3] * w[3][m])
            return carry

        lax.fori_loop(0, total // 8, body, 0)
    me = 2 * (b // 2) + s % 2
    width = rows + 2 * EDGE
    for rel, ref in enumerate((own, to_y, to_x, to_xy)):
        for quarter in range(4):

            @pl.when((me ^ rel) == quarter)
            def _(ref=ref, quarter=quarter):
                start = window_start(quarter, rows, total)
                ref[...] = part[:, :, start : start + width, :]


def sum_kernel(own, from_x, from_y, from_xy, pair, far, near, cross):
    y = lax.axis_index("slab") % 2
    c = lax.axis_index("bin") % 2
    for m in range(3):
        for layer in range(2):
            a = own[m, layer] + from_x[m, layer]
            d = from_y[m, layer] + from_xy[m, layer]
            pair[y, m, layer] = a
            pair[1 - y, m, layer] = d
    far[...] = pair[c]
    for m in range(3):
        near[m, 0] = pair[1 - c, m, 1 - c]

        @pl.when(c == 0)
        def _(m=m):
            cross[m, 0] = pair[0, m, 1]
            cross[m, 1] = pair[1, m, 0]
            cross[m, 2] = pair[1, m, 1]

        @pl.when(c == 1)
        def _(m=m):
            cross[m, 0] = pair[0, m, 0]
            cross[m, 1] = pair[0, m, 1]
            cross[m, 2] = pair[1, m, 0]


def place(dims):
    bins, rows, total, lanes, depth = dims
    b = lax.axis_index("bin")
    s = lax.axis_index("slab")
    c = b % 2
    return c, 2 * (b // 2) + s % 2, (s // 2) * 8 + 4 * c - 3


def layer_stepper(dims, att, pen, tvw, fields, dual, down):
    bins, rows, total, lanes, depth = dims
    tiles, columns = (rows + 2 * EDGE) // 8, lanes // 128
    c, me, z_base = place(dims)
    pen_value = pen[0]
    inv = normal_inverse(att, pen_value, bins)
    inv = [[pen_value * e for e in row] for row in inv]
    threshold = tvw[0] / pen_value
    squared = threshold * threshold
    lane = lax.broadcasted_iota(jnp.int32, (8, 128), 1)
    sub = lax.broadcasted_iota(jnp.int32, (8, 128), 0)
    last_lane, first_lane = lane == 127, lane == 0
    last_sub, first_sub = sub == 7, sub == 0
    at_end = last_sub & (me == 3)
    zero = jnp.zeros((8, 128), jnp.float32)

    def at(t, col):
        return slice(8 * t, 8 * t + 8), slice(128 * col, 128 * col + 128)

    def layer_step(i, turn):
        src, dst, first = fields[turn], fields[turn + 1], fields[0]
        final = turn == ITERS - 1
        to = i - 2 if final else i
        z = z_base + i
        z_inside = ((z >= 0) & (z < depth - 1)).astype(jnp.float32)

        def load(ref, m, layer, t, col):
            return ref[(m, layer) + at(t, col)]

        right = [None] * tiles
        for col in range(columns):
            below = None
            f = [load(src, m, i, 0, col) for m in range(3)]
            for t in range(tiles):
                following = None
                if t + 1 < tiles:
                    following = [load(src, m, i, t + 1, col) for m in range(3)]
                v = []
                for m in range(3):
                    gz = (load(src, m, i + 1, t, col) - f[m]) * z_inside
                    up = pltpu.roll(f[m], 7, 0)
                    if following is not None:
                        up = jnp.where(last_sub, pltpu.roll(following[m], 7, 0), up)
                    else:
                        up = jnp.where(at_end, f[m], up)
                    nxt = f[m]
                    if col + 1 < columns:
                        nxt = pltpu.roll(load(src, m, i, t, col + 1), 127, 1)
                    ahead = jnp.where(last_lane, nxt, pltpu.roll(f[m], 127, 1))
                    v.append([gz, up - f[m], ahead - f[m]])
                old = None
                if turn > 0:
                    old = [[load(dual, 3 * m + d, i, t, col) for d in range(3)] for m in range(3)]
                    v = [[v[m][d] + old[m][d] for d in range(3)] for m in range(3)]
                squares = [v[m][0] * v[m][0] + v[m][1] * v[m][1] + v[m][2] * v[m][2] for m in range(3)]
                scale = threshold * lax.rsqrt(jnp.maximum(squares[0] + squares[1] + squares[2], squared))
                if final:
                    scale = scale + scale
                fresh = [[v[m][d] * scale for d in range(3)] for m in range(3)]
                if not final:
                    for m in range(3):
                        for d in range(3):
                            dual[(3 * m + d, i) + at(t, col)] = fresh[m][d]
                if turn == 0:
                    step = fresh
                elif final:
                    step = [[fresh[m][d] - old[m][d] for d in range(3)] for m in range(3)]
                else:
                    step = [[(fresh[m][d] + fresh[m][d]) - old[m][d] for d in range(3)] for m in range(3)]
                lower = [down[(m,) + at(t, col)] for m in range(3)]
                for m in range(3):
                    down[(m,) + at(t, col)] = step[m][0]
                rolled_y = [pltpu.roll(step[m][1], 1, 0) for m in range(3)]
                rolled_x = [pltpu.roll(step[m][2], 1, 1) for m in range(3)]
                rhs = []
                for m in range(3):
                    prev_y = jnp.where(first_sub, zero if below is None else below[m], rolled_y[m])
                    prev_x = jnp.where(first_lane, zero if right[t] is None else right[t][m], rolled_x[m])
                    div = (step[m][0] - lower[m]) + (step[m][1] - prev_y) + (step[m][2] - prev_x)
                    if turn == 0:
                        div = div + div
                    rhs.append(12.0 * f[m] + div)
                below, right[t] = rolled_y, rolled_x
                for m in range(3):
                    dst[(m, to) + at(t, col)] = load(first, m, i, t, col) + (
                        inv[m][0] * rhs[0] + inv[m][1] * rhs[1] + inv[m][2] * rhs[2]
                    )
                f = following

    def run(start, count, turn):
        def body(i, carry):
            layer_step(start + i, turn)
            return carry

        lax.fori_loop(0, count, body, 0)

    def correct(i, turn):
        dst = fields[turn + 1]
        to = i - 2 if turn == ITERS - 1 else i
        for col in range(columns):
            for t in range(tiles):
                low = [down[(m,) + at(t, col)] for m in range(3)]
                if turn == 0:
                    low = [e + e for e in low]
                for m in range(3):
                    dst[(m, to) + at(t, col)] = dst[(m, to) + at(t, col)] - (
                        inv[m][0] * low[0] + inv[m][1] * low[1] + inv[m][2] * low[2]
                    )

    return run, correct


def inner_kernel(dims, att, pen, tvw, pair, cross, f0, f1, f2, f3, dual, kept, down):
    c, me, z_base = place(dims)

    @pl.when(c == 0)
    def _():
        f0[:, 3] = pair[0, :, 0]
        f0[:, 4] = pair[0, :, 1]
        f0[:, 5] = cross[:, 0]
        f0[:, 6] = cross[:, 1]
        f0[:, 7] = pair[1, :, 0]
        f0[:, 8] = pair[1, :, 1]
        f0[:, 9] = cross[:, 2]

    @pl.when(c == 1)
    def _():
        f0[:, 0] = cross[:, 0]
        f0[:, 1] = pair[0, :, 0]
        f0[:, 2] = pair[0, :, 1]
        f0[:, 3] = cross[:, 1]
        f0[:, 4] = cross[:, 2]
        f0[:, 5] = pair[1, :, 0]
        f0[:, 6] = pair[1, :, 1]

    run, correct = layer_stepper(dims, att, pen, tvw, (f0, f1, f2, f3), dual, down)
    for turn in range(ITERS):
        down[...] = jnp.zeros_like(down)
        run(jnp.where(c == 0, 3, 0) + turn, 6 - 2 * turn, turn)
        kept[turn] = down[...]


def outer_kernel(dims, att, pen, tvw, far, near, g0, g1, g2, g3, gd, kept, f0, f1, f2, f3, dual, o0, o1, o2, o3, down):
    bins, rows, total, lanes, depth = dims
    c, me, z_base = place(dims)

    @pl.when(c == 0)
    def _():
        f0[:, 0] = near[:, 0]
        f0[:, 1] = far[:, 0]
        f0[:, 2] = far[:, 1]

    @pl.when(c == 1)
    def _():
        f0[:, 7] = far[:, 0]
        f0[:, 8] = far[:, 1]
        f0[:, 9] = near[:, 0]

    run, correct = layer_stepper(dims, att, pen, tvw, (f0, f1, f2, f3), dual, down)
    for turn in range(ITERS):

        @pl.when(c == 0)
        def _():
            down[...] = jnp.zeros_like(down)

        @pl.when(c == 1)
        def _(turn=turn):
            down[...] = kept[turn]

        run(jnp.where(c == 0, turn, 6 - turn), 3, turn)

        @pl.when(c == 0)
        def _(turn=turn):
            correct(3 + turn, turn)

    outs = (o0, o1, o2, o3)
    for quarter in range(4):

        @pl.when(me == quarter)
        def _(quarter=quarter):
            start = rows * quarter - window_start(quarter, rows, total)
            for j in range(4):
                outs[j ^ quarter][...] = f3[:, 1 + j, start : start + rows, :]


def gather_kernel(rows, r0, r1, r2, r3, out):
    j = lax.axis_index("slab") % 4
    for t, ref in enumerate((r0, r1, r2, r3)):
        at = pl.multiple_of((j ^ t) * rows, 8)
        out[:, 0, pl.ds(at, rows), :] = ref[...]


def call(kernel, outs, args, smem=0, scratch=(), aliases=None, flops=0):
    shapes = [jax.ShapeDtypeStruct(o, jnp.float32) for o in outs]
    held = sum(math.prod(a.shape) for a in (*shapes, *args[smem:], *scratch))
    return pl.pallas_call(
        kernel,
        out_shape=shapes,
        in_specs=[pl.BlockSpec(memory_space=SMEM)] * smem
        + [pl.BlockSpec(memory_space=VMEM)] * (len(args) - smem),
        out_specs=[pl.BlockSpec(memory_space=VMEM)] * len(outs),
        scratch_shapes=list(scratch),
        input_output_aliases=aliases or {},
        cost_estimate=pl.CostEstimate(flops=flops, bytes_accessed=4 * held, transcendentals=0),
        compiler_params=pltpu.CompilerParams(vmem_limit_bytes=4 * held + (2 << 20)),
    )(*args)


def on_device(mesh_bin, mesh_slab, volumes, attenuation, penalty, tv_weight):
    own_bins, layers, total, lanes = volumes.shape
    bins = own_bins * mesh_bin
    assert mesh_bin == 4 and own_bins == 2 and layers == 4 and mesh_slab % 4 == 0
    rows = total // 4
    width = rows + 2 * EDGE
    depth = layers * mesh_slab
    devices = [(b, s) for b in range(mesh_bin) for s in range(mesh_slab)]

    def send(x, where):
        pairs = []
        for b, s in devices:
            to = where(b, s)
            if 0 <= to[0] < mesh_bin and 0 <= to[1] < mesh_slab:
                pairs.append((b * mesh_slab + s, to[0] * mesh_slab + to[1]))
        return lax.ppermute(x, ("bin", "slab"), pairs)

    c = lax.axis_index("bin") % 2
    away = lax.dynamic_slice_in_dim(volumes, 2 * (1 - c), 2, 1)
    mine = lax.dynamic_slice_in_dim(volumes, 2 * c, 2, 1)
    other = send(away, lambda b, s: (b ^ 1, s))

    win = (3, 2, width, lanes)
    own, to_x, to_y, to_xy = call(
        functools.partial(project_kernel, (bins, rows, total, lanes)),
        [win] * 4,
        (attenuation.T, penalty, mine, other),
        smem=2,
        scratch=[VMEM((3, 2, total, lanes), jnp.float32)],
    )
    from_xy = send(to_xy, lambda b, s: (b ^ 2, s ^ 1))
    from_x = send(to_x, lambda b, s: (b ^ 2, s))
    from_y = send(to_y, lambda b, s: (b, s ^ 1))
    pair, far, near, cross = call(
        sum_kernel,
        [(2,) + win, win, (3, 1, width, lanes), (3, 3, width, lanes)],
        (own, from_x, from_y, from_xy),
    )
    far = send(far, lambda b, s: (b ^ 1, s + (2 if b % 2 else -2)))
    near = send(near, lambda b, s: (b, s + (-2 if b % 2 else 2)))
    cross = send(cross, lambda b, s: (b ^ 1, s))
    dims = (bins, rows, total, lanes, depth)
    state = [(3, 10, width, lanes)] * 3 + [(3, 5, width, lanes), (9, 9, width, lanes)]
    kept = (3, 3, width, lanes)
    scalars = (attenuation.T, penalty, tv_weight)
    work = 150 * width * lanes
    inner = call(
        functools.partial(inner_kernel, dims),
        state + [kept],
        scalars + (pair, cross),
        smem=3,
        scratch=[VMEM((3, width, lanes), jnp.float32)],
        flops=12 * work,
    )
    blocks = call(
        functools.partial(outer_kernel, dims),
        state + [(3, rows, lanes)] * 4,
        (*scalars, far, near, *inner),
        smem=3,
        scratch=[VMEM((3, width, lanes), jnp.float32)],
        aliases={5 + i: i for i in range(5)},
        flops=9 * work,
    )[5:]

    def owner(t):
        def where(b, s):
            j = t ^ (2 * (b // 2) + s % 2)
            z = (s // 2) * 8 + 4 * (b % 2) + j
            return z // mesh_slab, z % mesh_slab

        return where

    blocks = [send(block, owner(t)) for t, block in enumerate(blocks)]
    return call(functools.partial(gather_kernel, rows), [(3, 1, total, lanes)], blocks)[0]


def solution(mesh):
    placed = (P("bin", "slab", None, None), P(), P(), P())
    return jax.shard_map(
        functools.partial(on_device, mesh.shape["bin"], mesh.shape["slab"]),
        mesh=mesh,
        in_specs=placed,
        out_specs=P(None, ("bin", "slab"), None, None),
        check_vma=False,
    )
```

```python
import functools
import math

import jax
import jax.numpy as jnp
from jax import lax
from jax.experimental import pallas as pl
from jax.experimental.pallas import tpu as pltpu
from jax.sharding import PartitionSpec as P

ITERS = 3
EDGE = 4
VMEM = pltpu.VMEM
SMEM = pltpu.SMEM


def window_start(quarter, rows, total):
    return min(max(rows * quarter - EDGE, 0), total - rows - 2 * EDGE)


def inverse_three(m):
    cof = [
        [
            m[(r + 1) % 3][(c + 1) % 3] * m[(r + 2) % 3][(c + 2) % 3]
            - m[(r + 1) % 3][(c + 2) % 3] * m[(r + 2) % 3][(c + 1) % 3]
            for c in range(3)
        ]
        for r in range(3)
    ]
    det = m[0][0] * cof[0][0] + m[0][1] * cof[0][1] + m[0][2] * cof[0][2]
    over = 1.0 / det
    return [[cof[c][r] * over for c in range(3)] for r in range(3)]


def normal_inverse(att, pen, bins):
    gram = [[None] * 3 for _ in range(3)]
    for i in range(3):
        for j in range(i, 3):
            total = att[i, 0] * att[j, 0]
            for k in range(1, bins):
                total = total + att[i, k] * att[j, k]
            gram[i][j] = gram[j][i] = total
    for i in range(3):
        gram[i][i] = gram[i][i] + 12.0 * pen
    return inverse_three(gram)


def ready_kernel(bins, att, pen, tvw, numbers):
    def put(at, value):
        numbers[at] = jnp.full((8, 128), value, jnp.float32)

    b = lax.axis_index("bin")
    inv = normal_inverse(att, pen[0], bins)
    for k in range(4):
        a = [att[m, (2 * b if k < 2 else 2 * (b ^ 1)) + k % 2] for m in range(3)]
        for m in range(3):
            put(3 * k + m, inv[m][0] * a[0] + inv[m][1] * a[1] + inv[m][2] * a[2])
    for m in range(3):
        for n in range(3):
            put(12 + 3 * m + n, pen[0] * inv[m][n])
    put(21, tvw[0] / pen[0])


def project_kernel(dims, numbers, mine, other, own, to_x, to_y, to_xy, part):
    bins, rows, total, lanes, depth = dims
    c, me, z_base = place(dims)
    w = [[numbers[3 * k + m] for m in range(3)] for k in range(4)]

    def body(t, carry):
        tile = pl.ds(pl.multiple_of(t * 8, 8), 8)
        for layer in range(2):
            for col in range(lanes // 128):
                at = (layer, tile, slice(128 * col, 128 * col + 128))
                v = [mine[(0, *at)], mine[(1, *at)], other[(0, *at)], other[(1, *at)]]
                for m in range(3):
                    part[(m, *at)] = v[0] * w[0][m] + v[1] * w[1][m] + (v[2] * w[2][m] + v[3] * w[3][m])
        return carry

    lax.fori_loop(0, total // 8, body, 0)
    width = rows + 2 * EDGE
    for rel, ref in enumerate((own, to_y, to_x, to_xy)):
        for quarter in range(4):

            @pl.when((me ^ rel) == quarter)
            def _(ref=ref, quarter=quarter):
                start = window_start(quarter, rows, total)
                ref[...] = part[:, :, start : start + width, :]


def sum_kernel(own, from_x, from_y, from_xy, f0, far, near, cross):
    y = lax.axis_index("slab") % 2
    c = lax.axis_index("bin") % 2
    for e in range(2):
        for m in range(3):
            f0[m, 3 + 4 * y - 2 * c + e] = own[m, e] + from_x[m, e]
            f0[m, 7 - 4 * y - 2 * c + e] = from_y[m, e] + from_xy[m, e]
    for core in range(2):

        @pl.when(c == core)
        def _(core=core):
            slab = [f0.at[:, 3 + 4 * k - 2 * core + e] for k in range(2) for e in range(2)]
            far[:, 0] = slab[2 * core][...]
            far[:, 1] = slab[2 * core + 1][...]
            near[:, 0] = slab[2 * (1 - core) + 1 - core][...]
            for at, k in enumerate(((1, 2, 3), (0, 1, 2))[core]):
                cross[:, at] = slab[k][...]


def place(dims):
    bins, rows, total, lanes, depth = dims
    b = lax.axis_index("bin")
    s = lax.axis_index("slab")
    c = b % 2
    return c, 2 * (b // 2) + s % 2, (s // 2) * 8 + 4 * c - 3


def layer_stepper(dims, numbers, fields, dual, down):
    bins, rows, total, lanes, depth = dims
    tiles, columns = (rows + 2 * EDGE) // 8, lanes // 128
    c, me, z_base = place(dims)
    inv = [[numbers[12 + 3 * m + n] for n in range(3)] for m in range(3)]
    threshold = numbers[21]
    squared = threshold * threshold
    lane = lax.broadcasted_iota(jnp.int32, (8, 128), 1)
    sub = lax.broadcasted_iota(jnp.int32, (8, 128), 0)
    last_lane, first_lane = lane == 127, lane == 0
    last_sub, first_sub = sub == 7, sub == 0
    at_end = last_sub & (me == 3)
    zero = jnp.zeros((8, 128), jnp.float32)

    def at(t, col):
        return slice(8 * t, 8 * t + 8), slice(128 * col, 128 * col + 128)

    def layer_step(i, turn):
        src, dst, first = fields[turn], fields[turn + 1], fields[0]
        final = turn == ITERS - 1
        to = i - 2 if final else i
        z = z_base + i
        z_inside = ((z >= 0) & (z < depth - 1)).astype(jnp.float32)

        def load(ref, m, layer, t, col):
            return ref[(m, layer) + at(t, col)]

        right = [None] * tiles
        for col in range(columns):
            below = None
            f = [load(src, m, i, 0, col) for m in range(3)]
            for t in range(tiles):
                following = None
                if t + 1 < tiles:
                    following = [load(src, m, i, t + 1, col) for m in range(3)]
                v = []
                for m in range(3):
                    gz = (load(src, m, i + 1, t, col) - f[m]) * z_inside
                    up = pltpu.roll(f[m], 7, 0)
                    if following is not None:
                        up = jnp.where(last_sub, pltpu.roll(following[m], 7, 0), up)
                    else:
                        up = jnp.where(at_end, f[m], up)
                    nxt = f[m]
                    if col + 1 < columns:
                        nxt = pltpu.roll(load(src, m, i, t, col + 1), 127, 1)
                    ahead = jnp.where(last_lane, nxt, pltpu.roll(f[m], 127, 1))
                    v.append([gz, up - f[m], ahead - f[m]])
                old = None
                if turn > 0:
                    old = [[load(dual, 3 * m + d, i, t, col) for d in range(3)] for m in range(3)]
                    v = [[v[m][d] + old[m][d] for d in range(3)] for m in range(3)]
                squares = [v[m][0] * v[m][0] + v[m][1] * v[m][1] + v[m][2] * v[m][2] for m in range(3)]
                scale = threshold * lax.rsqrt(jnp.maximum(squares[0] + squares[1] + squares[2], squared))
                if final:
                    scale = scale + scale
                fresh = [[v[m][d] * scale for d in range(3)] for m in range(3)]
                if not final:
                    for m in range(3):
                        for d in range(3):
                            dual[(3 * m + d, i) + at(t, col)] = fresh[m][d]
                if turn == 0:
                    step = fresh
                elif final:
                    step = [[fresh[m][d] - old[m][d] for d in range(3)] for m in range(3)]
                else:
                    step = [[(fresh[m][d] + fresh[m][d]) - old[m][d] for d in range(3)] for m in range(3)]
                lower = [down[(m,) + at(t, col)] for m in range(3)]
                for m in range(3):
                    down[(m,) + at(t, col)] = step[m][0]
                rolled_y = [pltpu.roll(step[m][1], 1, 0) for m in range(3)]
                rolled_x = [pltpu.roll(step[m][2], 1, 1) for m in range(3)]
                rhs = []
                for m in range(3):
                    prev_y = jnp.where(first_sub, zero if below is None else below[m], rolled_y[m])
                    prev_x = jnp.where(first_lane, zero if right[t] is None else right[t][m], rolled_x[m])
                    div = (step[m][0] - lower[m]) + (step[m][1] - prev_y) + (step[m][2] - prev_x)
                    if turn == 0:
                        div = div + div
                    rhs.append(12.0 * f[m] + div)
                below, right[t] = rolled_y, rolled_x
                for m in range(3):
                    dst[(m, to) + at(t, col)] = load(first, m, i, t, col) + (
                        inv[m][0] * rhs[0] + inv[m][1] * rhs[1] + inv[m][2] * rhs[2]
                    )
                f = following

    def run(start, count, turn):
        def body(i, carry):
            layer_step(start + i, turn)
            return carry

        lax.fori_loop(0, count, body, 0)

    def correct(i, turn):
        dst = fields[turn + 1]
        to = i - 2 if turn == ITERS - 1 else i
        for col in range(columns):
            for t in range(tiles):
                low = [down[(m,) + at(t, col)] for m in range(3)]
                if turn == 0:
                    low = [e + e for e in low]
                for m in range(3):
                    dst[(m, to) + at(t, col)] = dst[(m, to) + at(t, col)] - (
                        inv[m][0] * low[0] + inv[m][1] * low[1] + inv[m][2] * low[2]
                    )

    return run, correct


def inner_kernel(dims, numbers, cross, held, f0, f1, f2, f3, dual, kept, down):
    c, me, z_base = place(dims)
    for core in range(2):

        @pl.when(c == core)
        def _(core=core):
            for k, to in enumerate(((5, 6, 9), (0, 3, 4))[core]):
                f0[:, to] = cross[:, k]

    run, correct = layer_stepper(dims, numbers, (f0, f1, f2, f3), dual, down)
    for turn in range(ITERS):
        down[...] = jnp.zeros_like(down)
        run(jnp.where(c == 0, 3, 0) + turn, 6 - 2 * turn, turn)
        kept[turn] = down[...]


def outer_kernel(dims, numbers, far, near, g0, g1, g2, g3, gd, kept, f0, f1, f2, f3, dual, o0, o1, o2, o3, down):
    bins, rows, total, lanes, depth = dims
    c, me, z_base = place(dims)
    for core in range(2):

        @pl.when(c == core)
        def _(core=core):
            for k, to in enumerate(((1, 2, 0), (7, 8, 9))[core]):
                f0[:, to] = far[:, k] if k < 2 else near[:, 0]

    run, correct = layer_stepper(dims, numbers, (f0, f1, f2, f3), dual, down)
    for turn in range(ITERS):

        @pl.when(c == 0)
        def _():
            down[...] = jnp.zeros_like(down)

        @pl.when(c == 1)
        def _(turn=turn):
            down[...] = kept[turn]

        run(jnp.where(c == 0, turn, 6 - turn), 3, turn)

        @pl.when(c == 0)
        def _(turn=turn):
            correct(3 + turn, turn)

    outs = (o0, o1, o2, o3)
    twist = twist_of(c, lax.axis_index("slab") // 2, lax.axis_size("slab"))
    for quarter in range(4):
        for turned in (0, 2):

            @pl.when((me == quarter) & (twist == turned))
            def _(quarter=quarter, turned=turned):
                start = rows * quarter - window_start(quarter, rows, total)
                for j in range(4):
                    outs[j ^ quarter ^ turned][...] = f3[:, 1 + j, start : start + rows, :]


def twist_of(core, plane, slabs):
    return 2 * ((core + plane // (slabs // 4)) % 2)


def gather_kernel(rows, r0, r1, r2, r3, out):
    slabs = lax.axis_size("slab")
    z = lax.axis_index("bin") * slabs + lax.axis_index("slab")
    twist = twist_of(z // 4 % 2, z // 8, slabs)
    for t, ref in enumerate((r0, r1, r2, r3)):
        at = pl.multiple_of((z % 4 ^ t ^ twist) * rows, 8)
        out[:, 0, pl.ds(at, rows), :] = ref[...]


def call(kernel, outs, args, spaces=None, scratch=(), aliases=None, flops=0):
    shapes = [jax.ShapeDtypeStruct(o, jnp.float32) for o in outs]
    spaces = spaces or [VMEM] * len(args)
    held = sum(math.prod(a.shape) for a in (*shapes, *args, *scratch))
    return pl.pallas_call(
        kernel,
        out_shape=shapes,
        in_specs=[pl.BlockSpec(memory_space=m) for m in spaces],
        out_specs=[pl.BlockSpec(memory_space=m) for m in [VMEM] * len(outs)],
        scratch_shapes=list(scratch),
        input_output_aliases=aliases or {},
        cost_estimate=pl.CostEstimate(flops=flops, bytes_accessed=4 * held, transcendentals=0),
        compiler_params=pltpu.CompilerParams(vmem_limit_bytes=4 * held + (2 << 20)),
    )(*args)


def on_device(mesh_bin, mesh_slab, volumes, attenuation, penalty, tv_weight):
    own_bins, layers, total, lanes = volumes.shape
    bins = own_bins * mesh_bin
    assert mesh_bin == 4 and own_bins == 2 and layers == 4 and mesh_slab % 4 == 0
    rows = total // 4
    width = rows + 2 * EDGE
    depth = layers * mesh_slab
    devices = [(b, s) for b in range(mesh_bin) for s in range(mesh_slab)]

    def send(x, where):
        pairs = []
        for b, s in devices:
            to = where(b, s)
            if 0 <= to[0] < mesh_bin and 0 <= to[1] < mesh_slab:
                pairs.append((b * mesh_slab + s, to[0] * mesh_slab + to[1]))
        return lax.ppermute(x, ("bin", "slab"), pairs)

    dims = (bins, rows, total, lanes, depth)
    c = lax.axis_index("bin") % 2
    away = lax.dynamic_slice_in_dim(volumes, 2 * (1 - c), 2, 1)
    mine = lax.dynamic_slice_in_dim(volumes, 2 * c, 2, 1)
    other = send(away, lambda b, s: (b ^ 1, s))
    numbers = call(
        functools.partial(ready_kernel, bins),
        [(22, 8, 128)],
        (attenuation.T, penalty, tv_weight),
        [SMEM] * 3,
    )[0]
    win = (3, 2, width, lanes)
    own, to_x, to_y, to_xy = call(
        functools.partial(project_kernel, dims),
        [win] * 4,
        (numbers, mine, other),
        None,
        [VMEM((3, 2, total, lanes), jnp.float32)],
    )
    from_xy = send(to_xy, lambda b, s: (b ^ 2, s ^ 1))
    from_x = send(to_x, lambda b, s: (b ^ 2, s))
    from_y = send(to_y, lambda b, s: (b, s ^ 1))
    state = [(3, 10, width, lanes)] * 3 + [(3, 5, width, lanes), (9, 9, width, lanes)]
    f0, far, near, cross = call(
        sum_kernel,
        [state[0], win, (3, 1, width, lanes), (3, 3, width, lanes)],
        (own, from_x, from_y, from_xy),
    )
    far = send(far, lambda b, s: (b ^ 1, s + (2 if b % 2 else -2)))
    near = send(near, lambda b, s: (b, s + (-2 if b % 2 else 2)))
    cross = send(cross, lambda b, s: (b ^ 1, s))
    work = 150 * width * lanes
    scratch = [VMEM((3, width, lanes), jnp.float32)]
    inner = call(
        functools.partial(inner_kernel, dims),
        state + [(3, 3, width, lanes)],
        (numbers, cross, f0),
        None,
        scratch,
        {2: 0},
        12 * work,
    )
    blocks = call(
        functools.partial(outer_kernel, dims),
        state + [(3, rows, lanes)] * 4,
        (numbers, far, near, *inner),
        None,
        scratch,
        {3 + i: i for i in range(5)},
        9 * work,
    )[5:]

    def owner(t):
        def where(b, s):
            j = t ^ (2 * (b // 2) + s % 2) ^ twist_of(b % 2, s // 2, mesh_slab)
            z = (s // 2) * 8 + 4 * (b % 2) + j
            return z // mesh_slab, z % mesh_slab

        return where

    blocks = [send(block, owner(t)) for t, block in enumerate(blocks)]
    return call(functools.partial(gather_kernel, rows), [(3, 1, total, lanes)], blocks)[0]


def solution(mesh):
    placed = (P("bin", "slab", None, None), P(), P(), P())
    return jax.shard_map(
        functools.partial(on_device, mesh.shape["bin"], mesh.shape["slab"]),
        mesh=mesh,
        in_specs=placed,
        out_specs=P(None, ("bin", "slab"), None, None),
        check_vma=False,
    )
```

```python
import functools
import math

import jax
import jax.numpy as jnp
from jax import lax
from jax.experimental import pallas as pl
from jax.experimental.pallas import tpu as pltpu
from jax.sharding import PartitionSpec as P

ITERS = 3
EDGE = 4
ROUNDS = (1, 3, 0, 2)
TWIST = 0
VMEM = pltpu.VMEM


def window_start(quarter, rows, total):
    return min(max(rows * quarter - EDGE, 0), total - rows - 2 * EDGE)


def inverse_three(m):
    cof = [
        [
            m[(r + 1) % 3][(c + 1) % 3] * m[(r + 2) % 3][(c + 2) % 3]
            - m[(r + 1) % 3][(c + 2) % 3] * m[(r + 2) % 3][(c + 1) % 3]
            for c in range(3)
        ]
        for r in range(3)
    ]
    det = m[0][0] * cof[0][0] + m[0][1] * cof[0][1] + m[0][2] * cof[0][2]
    over = 1.0 / det
    return [[cof[c][r] * over for c in range(3)] for r in range(3)]


def away_kernel(volumes, away):
    c = lax.axis_index("bin") % 2
    for k in range(2):
        for layer in range(2):
            away[k, layer] = volumes[k, 2 * (1 - c) + layer]


def spread(x):
    return jnp.broadcast_to(x, (8, 128))


def spread_attenuation(att, bins):
    return [[spread(att[m : m + 1, k : k + 1]) for k in range(bins)] for m in range(3)]


def ready_kernel(bins, pen, tvw, att, numbers):
    a = spread_attenuation(att, bins)
    pen_value = spread(pen[...].reshape(1, 1))
    gram = [[None] * 3 for _ in range(3)]
    for i in range(3):
        for j in range(i, 3):
            total = a[i][0] * a[j][0]
            for k in range(1, bins):
                total = total + a[i][k] * a[j][k]
            gram[i][j] = gram[j][i] = total
    for i in range(3):
        gram[i][i] = gram[i][i] + 12.0 * pen_value
    inv = inverse_three(gram)
    for m in range(3):
        for n in range(3):
            numbers[3 * m + n] = inv[m][n]
            numbers[9 + 3 * m + n] = pen_value * inv[m][n]
    numbers[18] = spread(tvw[...].reshape(1, 1)) / pen_value


def project_kernel(dims, att, volumes, other, own, to_x, to_y, to_xy, part):
    bins, rows, total, lanes, depth = dims
    c, me, z_base = place(dims)
    b = lax.axis_index("bin")
    a = spread_attenuation(att, bins)
    w = []
    for k in range(4):
        group = b if k < 2 else b ^ 1
        row = []
        for m in range(3):
            value = a[m][k % 2]
            for g in range(1, bins // 2):
                value = jnp.where(group == g, a[m][2 * g + k % 2], value)
            row.append(value)
        w.append(row)

    def body(t, carry):
        tile = pl.ds(pl.multiple_of(t * 8, 8), 8)
        for layer in range(2):
            for col in range(lanes // 128):
                at = (layer, tile, slice(128 * col, 128 * col + 128))
                here = (2 * c + layer, *at[1:])
                v = [volumes[(0, *here)], volumes[(1, *here)], other[(0, *at)], other[(1, *at)]]
                for m in range(3):
                    part[(m, *at)] = v[0] * w[0][m] + v[1] * w[1][m] + (v[2] * w[2][m] + v[3] * w[3][m])
        return carry

    lax.fori_loop(0, total // 8, body, 0)
    width = rows + 2 * EDGE
    for rel, ref in enumerate((own, to_y, to_x, to_xy)):
        for quarter in range(4):

            @pl.when((me ^ rel) == quarter)
            def _(ref=ref, quarter=quarter):
                start = window_start(quarter, rows, total)
                ref[...] = part[:, :, start : start + width, :]


def sum_kernel(dims, numbers, own, from_x, from_y, from_xy, f0, far, near, cross):
    y = lax.axis_index("slab") % 2
    c = lax.axis_index("bin") % 2
    bins, rows, total, lanes, depth = dims
    inv = [[numbers[3 * m + n] for n in range(3)] for m in range(3)]
    for e in range(2):
        for to, one, two in ((3 + 4 * y, own, from_x), (7 - 4 * y, from_y, from_xy)):
            for t in range((rows + 2 * EDGE) // 8):
                for col in range(lanes // 128):
                    at = (slice(8 * t, 8 * t + 8), slice(128 * col, 128 * col + 128))
                    d = [one[(m, e, *at)] + two[(m, e, *at)] for m in range(3)]
                    for m in range(3):
                        f0[(m, to - 2 * c + e, *at)] = inv[m][0] * d[0] + inv[m][1] * d[1] + inv[m][2] * d[2]
    for core in range(2):

        @pl.when(c == core)
        def _(core=core):
            slab = [f0.at[:, 3 + 4 * k - 2 * core + e] for k in range(2) for e in range(2)]
            far[:, 0] = slab[2 * core][...]
            far[:, 1] = slab[2 * core + 1][...]
            near[:, 0] = slab[2 * (1 - core) + 1 - core][...]
            for at, k in enumerate(((1, 2, 3), (0, 1, 2))[core]):
                cross[:, at] = slab[k][...]


def place(dims):
    bins, rows, total, lanes, depth = dims
    b = lax.axis_index("bin")
    s = lax.axis_index("slab")
    c = b % 2
    return c, 2 * (b // 2) + s % 2, (s // 2) * 8 + 4 * c - 3


def layer_stepper(dims, numbers, fields, dual, down):
    bins, rows, total, lanes, depth = dims
    tiles, columns = (rows + 2 * EDGE) // 8, lanes // 128
    c, me, z_base = place(dims)
    inv = [[numbers[9 + 3 * m + n] for n in range(3)] for m in range(3)]
    threshold = numbers[18]
    squared = threshold * threshold
    lane = lax.broadcasted_iota(jnp.int32, (8, 128), 1)
    sub = lax.broadcasted_iota(jnp.int32, (8, 128), 0)
    last_lane, first_lane = lane == 127, lane == 0
    last_sub, first_sub = sub == 7, sub == 0
    at_end = last_sub & (me == 3)
    zero = jnp.zeros((8, 128), jnp.float32)

    def at(t, col):
        return slice(8 * t, 8 * t + 8), slice(128 * col, 128 * col + 128)

    def layer_step(i, turn):
        src, dst, first = fields[turn], fields[turn + 1], fields[0]
        final = turn == ITERS - 1
        to = i - 2 if final else i
        z = z_base + i
        z_inside = ((z >= 0) & (z < depth - 1)).astype(jnp.float32)

        def load(ref, m, layer, t, col):
            return ref[(m, layer) + at(t, col)]

        right = [None] * tiles
        for col in range(columns):
            below = None
            f = [load(src, m, i, 0, col) for m in range(3)]
            for t in range(tiles):
                following = None
                if t + 1 < tiles:
                    following = [load(src, m, i, t + 1, col) for m in range(3)]
                v = []
                for m in range(3):
                    gz = (load(src, m, i + 1, t, col) - f[m]) * z_inside
                    up = pltpu.roll(f[m], 7, 0)
                    if following is not None:
                        up = jnp.where(last_sub, pltpu.roll(following[m], 7, 0), up)
                    else:
                        up = jnp.where(at_end, f[m], up)
                    nxt = f[m]
                    if col + 1 < columns:
                        nxt = pltpu.roll(load(src, m, i, t, col + 1), 127, 1)
                    ahead = jnp.where(last_lane, nxt, pltpu.roll(f[m], 127, 1))
                    v.append([gz, up - f[m], ahead - f[m]])
                old = None
                if turn > 0:
                    old = [[load(dual, 3 * m + d, i, t, col) for d in range(3)] for m in range(3)]
                    v = [[v[m][d] + old[m][d] for d in range(3)] for m in range(3)]
                squares = [v[m][0] * v[m][0] + v[m][1] * v[m][1] + v[m][2] * v[m][2] for m in range(3)]
                scale = threshold * lax.rsqrt(jnp.maximum(squares[0] + squares[1] + squares[2], squared))
                if final:
                    scale = scale + scale
                fresh = [[v[m][d] * scale for d in range(3)] for m in range(3)]
                if not final:
                    for m in range(3):
                        for d in range(3):
                            dual[(3 * m + d, i) + at(t, col)] = fresh[m][d]
                if turn == 0:
                    step = fresh
                elif final:
                    step = [[fresh[m][d] - old[m][d] for d in range(3)] for m in range(3)]
                else:
                    step = [[(fresh[m][d] + fresh[m][d]) - old[m][d] for d in range(3)] for m in range(3)]
                lower = [down[(m,) + at(t, col)] for m in range(3)]
                for m in range(3):
                    down[(m,) + at(t, col)] = step[m][0]
                rolled_y = [pltpu.roll(step[m][1], 1, 0) for m in range(3)]
                rolled_x = [pltpu.roll(step[m][2], 1, 1) for m in range(3)]
                rhs = []
                for m in range(3):
                    prev_y = jnp.where(first_sub, zero if below is None else below[m], rolled_y[m])
                    prev_x = jnp.where(first_lane, zero if right[t] is None else right[t][m], rolled_x[m])
                    div = (step[m][0] - lower[m]) + (step[m][1] - prev_y) + (step[m][2] - prev_x)
                    if turn == 0:
                        div = div + div
                    rhs.append(12.0 * f[m] + div)
                below, right[t] = rolled_y, rolled_x
                for m in range(3):
                    dst[(m, to) + at(t, col)] = load(first, m, i, t, col) + (
                        inv[m][0] * rhs[0] + inv[m][1] * rhs[1] + inv[m][2] * rhs[2]
                    )
                f = following

    def run(start, count, turn):
        def body(i, carry):
            layer_step(start + i, turn)
            return carry

        lax.fori_loop(0, count, body, 0)

    def correct(i, turn):
        dst = fields[turn + 1]
        to = i - 2 if turn == ITERS - 1 else i
        for col in range(columns):
            for t in range(tiles):
                low = [down[(m,) + at(t, col)] for m in range(3)]
                if turn == 0:
                    low = [e + e for e in low]
                for m in range(3):
                    dst[(m, to) + at(t, col)] = dst[(m, to) + at(t, col)] - (
                        inv[m][0] * low[0] + inv[m][1] * low[1] + inv[m][2] * low[2]
                    )

    return run, correct


def inner_kernel(dims, numbers, cross, held, f0, f1, f2, f3, dual, kept, down):
    c, me, z_base = place(dims)
    for core in range(2):

        @pl.when(c == core)
        def _(core=core):
            for k, to in enumerate(((5, 6, 9), (0, 3, 4))[core]):
                f0[:, to] = cross[:, k]

    run, correct = layer_stepper(dims, numbers, (f0, f1, f2, f3), dual, down)
    for turn in range(ITERS):
        down[...] = jnp.zeros_like(down)
        run(jnp.where(c == 0, 3, 0) + turn, 6 - 2 * turn, turn)
        kept[turn] = down[...]


def outer_kernel(dims, numbers, far, near, g0, g1, g2, g3, gd, kept, f0, f1, f2, f3, dual, o0, o1, o2, o3, down):
    bins, rows, total, lanes, depth = dims
    c, me, z_base = place(dims)
    for core in range(2):

        @pl.when(c == core)
        def _(core=core):
            for k, to in enumerate(((1, 2, 0), (7, 8, 9))[core]):
                f0[:, to] = far[:, k] if k < 2 else near[:, 0]

    run, correct = layer_stepper(dims, numbers, (f0, f1, f2, f3), dual, down)
    for turn in range(ITERS):

        @pl.when(c == 0)
        def _():
            down[...] = jnp.zeros_like(down)

        @pl.when(c == 1)
        def _(turn=turn):
            down[...] = kept[turn]

        run(jnp.where(c == 0, turn, 6 - turn), 3, turn)

        @pl.when(c == 0)
        def _(turn=turn):
            correct(3 + turn, turn)

    outs = (o0, o1, o2, o3)
    twist = twist_of(c, lax.axis_index("slab") // 2, lax.axis_size("slab"))
    for quarter in range(4):
        for turned in {0, TWIST}:

            @pl.when((me == quarter) & (twist == turned))
            def _(quarter=quarter, turned=turned):
                start = rows * quarter - window_start(quarter, rows, total)
                for j in range(4):
                    outs[ROUNDS.index(j ^ quarter ^ turned)][...] = f3[:, 1 + j, start : start + rows, :]


def twist_of(core, plane, slabs):
    return TWIST * ((core + plane // (slabs // 4)) % 2)


def gather_kernel(rows, r0, r1, r2, r3, out, sem):
    slabs = lax.axis_size("slab")
    z = lax.axis_index("bin") * slabs + lax.axis_index("slab")
    twist = twist_of(z // 4 % 2, z // 8, slabs)
    copies = []
    for n, (t, ref) in enumerate(zip(ROUNDS, (r0, r1, r2, r3))):
        at = pl.multiple_of((z % 4 ^ t ^ twist) * rows, 8)
        copies.append(pltpu.make_async_copy(ref, out.at[:, 0, pl.ds(at, rows), :], sem.at[n]))
        copies[-1].start()
    for copy in copies:
        copy.wait()


def call(kernel, outs, args, spaces=None, scratch=(), aliases=None, flops=0, out_space=VMEM):
    shapes = [jax.ShapeDtypeStruct(o, jnp.float32) for o in outs]
    spaces = spaces or [VMEM] * len(args)
    held = sum(math.prod(a.shape) for a in (*shapes, *args, *scratch))
    return pl.pallas_call(
        kernel,
        out_shape=shapes,
        in_specs=[pl.BlockSpec(memory_space=m) for m in spaces],
        out_specs=[pl.BlockSpec(memory_space=m) for m in [out_space] * len(outs)],
        scratch_shapes=list(scratch),
        input_output_aliases=aliases or {},
        cost_estimate=pl.CostEstimate(flops=flops, bytes_accessed=4 * held, transcendentals=0),
        compiler_params=pltpu.CompilerParams(vmem_limit_bytes=4 * held + (2 << 20)),
    )(*args)


def on_device(mesh_bin, mesh_slab, volumes, attenuation, penalty, tv_weight):
    own_bins, layers, total, lanes = volumes.shape
    bins = own_bins * mesh_bin
    assert mesh_bin == 4 and own_bins == 2 and layers == 4 and mesh_slab % 4 == 0
    rows = total // 4
    width = rows + 2 * EDGE
    depth = layers * mesh_slab
    devices = [(b, s) for b in range(mesh_bin) for s in range(mesh_slab)]

    def send(x, where):
        pairs = []
        for b, s in devices:
            to = where(b, s)
            if 0 <= to[0] < mesh_bin and 0 <= to[1] < mesh_slab:
                pairs.append((b * mesh_slab + s, to[0] * mesh_slab + to[1]))
        return lax.ppermute(x, ("bin", "slab"), pairs)

    dims = (bins, rows, total, lanes, depth)
    away = call(away_kernel, [(2, 2, total, lanes)], (volumes,))[0]
    other = send(away, lambda b, s: (b ^ 1, s))
    win = (3, 2, width, lanes)
    own, to_x, to_y, to_xy = call(
        functools.partial(project_kernel, dims),
        [win] * 4,
        (attenuation.T, volumes, other),
        None,
        [VMEM((3, 2, total, lanes), jnp.float32)],
    )
    from_xy = send(to_xy, lambda b, s: (b ^ 2, s ^ 1))
    from_x = send(to_x, lambda b, s: (b ^ 2, s))
    from_y = send(to_y, lambda b, s: (b, s ^ 1))
    numbers = call(
        functools.partial(ready_kernel, bins), [(19, 8, 128)], (penalty, tv_weight, attenuation.T)
    )[0]
    state = [(3, 10, width, lanes)] * 3 + [(3, 5, width, lanes), (9, 9, width, lanes)]
    f0, far, near, cross = call(
        functools.partial(sum_kernel, dims),
        [state[0], win, (3, 1, width, lanes), (3, 3, width, lanes)],
        (numbers, own, from_x, from_y, from_xy),
    )
    far = send(far, lambda b, s: (b ^ 1, s + (2 if b % 2 else -2)))
    near = send(near, lambda b, s: (b, s + (-2 if b % 2 else 2)))
    cross = send(cross, lambda b, s: (b ^ 1, s))
    work = 150 * width * lanes
    scratch = [VMEM((3, width, lanes), jnp.float32)]
    inner = call(
        functools.partial(inner_kernel, dims),
        state + [(3, 3, width, lanes)],
        (numbers, cross, f0),
        None,
        scratch,
        {2: 0},
        12 * work,
    )
    blocks = call(
        functools.partial(outer_kernel, dims),
        state + [(3, rows, lanes)] * 4,
        (numbers, far, near, *inner),
        None,
        scratch,
        {3 + i: i for i in range(5)},
        9 * work,
    )[5:]

    def owner(t):
        def where(b, s):
            j = t ^ (2 * (b // 2) + s % 2) ^ twist_of(b % 2, s // 2, mesh_slab)
            z = (s // 2) * 8 + 4 * (b % 2) + j
            return z // mesh_slab, z % mesh_slab

        return where

    blocks = [send(block, owner(key)) for key, block in zip(ROUNDS, blocks)]
    return call(
        functools.partial(gather_kernel, rows),
        [(3, 1, total, lanes)],
        blocks,
        scratch=[pltpu.SemaphoreType.DMA((4,))],
        out_space=pl.ANY,
    )[0]


def solution(mesh):
    placed = (P("bin", "slab", None, None), P(), P(), P())
    return jax.shard_map(
        functools.partial(on_device, mesh.shape["bin"], mesh.shape["slab"]),
        mesh=mesh,
        in_specs=placed,
        out_specs=P(None, ("bin", "slab"), None, None),
        check_vma=False,
    )
```

```python
import functools
import math

import jax
import jax.numpy as jnp
from jax import lax
from jax.experimental import pallas as pl
from jax.experimental.pallas import tpu as pltpu
from jax.sharding import PartitionSpec as P

ITERS = 3
EDGE = 4
ROUNDS = (1, 3, 0, 2)
TWIST = 0
VMEM = pltpu.VMEM


def window_start(quarter, rows, total):
    return min(max(rows * quarter - EDGE, 0), total - rows - 2 * EDGE)


def inverse_three(m):
    cof = [
        [
            m[(r + 1) % 3][(c + 1) % 3] * m[(r + 2) % 3][(c + 2) % 3]
            - m[(r + 1) % 3][(c + 2) % 3] * m[(r + 2) % 3][(c + 1) % 3]
            for c in range(3)
        ]
        for r in range(3)
    ]
    det = m[0][0] * cof[0][0] + m[0][1] * cof[0][1] + m[0][2] * cof[0][2]
    over = 1.0 / det
    return [[cof[c][r] * over for c in range(3)] for r in range(3)]


def away_kernel(volumes, first, second):
    c = lax.axis_index("bin") % 2
    for e, ref in enumerate((first, second)):
        for k in range(2):
            ref[k] = volumes[k, 2 * (1 - c) + e]


def spread(x):
    return jnp.broadcast_to(x, (8, 128))


def spread_attenuation(att, bins):
    return [[spread(att[m : m + 1, k : k + 1]) for k in range(bins)] for m in range(3)]


def ready_kernel(bins, pen, tvw, att, numbers):
    a = spread_attenuation(att, bins)
    pen_value = spread(pen[...].reshape(1, 1))
    gram = [[None] * 3 for _ in range(3)]
    for i in range(3):
        for j in range(i, 3):
            total = a[i][0] * a[j][0]
            for k in range(1, bins):
                total = total + a[i][k] * a[j][k]
            gram[i][j] = gram[j][i] = total
    for i in range(3):
        gram[i][i] = gram[i][i] + 12.0 * pen_value
    inv = inverse_three(gram)
    for m in range(3):
        for n in range(3):
            numbers[3 * m + n] = inv[m][n]
            numbers[9 + 3 * m + n] = pen_value * inv[m][n]
    numbers[18] = spread(tvw[...].reshape(1, 1)) / pen_value


def project_kernel(dims, e, att, volumes, other, own, to_x, to_y, to_xy, part):
    bins, rows, total, lanes, depth = dims
    c, me, z_base = place(dims)
    b = lax.axis_index("bin")
    a = spread_attenuation(att, bins)
    w = []
    for k in range(4):
        group = b if k < 2 else b ^ 1
        row = []
        for m in range(3):
            value = a[m][k % 2]
            for g in range(1, bins // 2):
                value = jnp.where(group == g, a[m][2 * g + k % 2], value)
            row.append(value)
        w.append(row)

    def body(t, carry):
        tile = pl.ds(pl.multiple_of(t * 8, 8), 8)
        for col in range(lanes // 128):
            at = (tile, slice(128 * col, 128 * col + 128))
            v = [volumes[(0, 2 * c + e, *at)], volumes[(1, 2 * c + e, *at)], other[(0, *at)], other[(1, *at)]]
            for m in range(3):
                part[(m, *at)] = v[0] * w[0][m] + v[1] * w[1][m] + (v[2] * w[2][m] + v[3] * w[3][m])
        return carry

    lax.fori_loop(0, total // 8, body, 0)
    width = rows + 2 * EDGE
    for rel, ref in enumerate((own, to_y, to_x, to_xy)):
        for quarter in range(4):

            @pl.when((me ^ rel) == quarter)
            def _(ref=ref, quarter=quarter):
                start = window_start(quarter, rows, total)
                ref[...] = part[:, start : start + width, :]


def sum_kernel(dims, numbers, *refs):
    parts, (f0, far, near, cross) = (refs[:4], refs[4:8]), refs[8:]
    y = lax.axis_index("slab") % 2
    c = lax.axis_index("bin") % 2
    bins, rows, total, lanes, depth = dims
    inv = [[numbers[3 * m + n] for n in range(3)] for m in range(3)]
    for e in range(2):
        own, from_x, from_y, from_xy = parts[e]
        for to, one, two in ((3 + 4 * y, own, from_x), (7 - 4 * y, from_y, from_xy)):
            for t in range((rows + 2 * EDGE) // 8):
                for col in range(lanes // 128):
                    at = (slice(8 * t, 8 * t + 8), slice(128 * col, 128 * col + 128))
                    d = [one[(m, *at)] + two[(m, *at)] for m in range(3)]
                    for m in range(3):
                        f0[(m, to - 2 * c + e, *at)] = inv[m][0] * d[0] + inv[m][1] * d[1] + inv[m][2] * d[2]
    for core in range(2):

        @pl.when(c == core)
        def _(core=core):
            slab = [f0.at[:, 3 + 4 * k - 2 * core + e] for k in range(2) for e in range(2)]
            far[:, 0] = slab[2 * core][...]
            far[:, 1] = slab[2 * core + 1][...]
            near[:, 0] = slab[2 * (1 - core) + 1 - core][...]
            for at, k in enumerate(((1, 2, 3), (0, 1, 2))[core]):
                cross[:, at] = slab[k][...]


def place(dims):
    bins, rows, total, lanes, depth = dims
    b = lax.axis_index("bin")
    s = lax.axis_index("slab")
    c = b % 2
    return c, 2 * (b // 2) + s % 2, (s // 2) * 8 + 4 * c - 3


def layer_stepper(dims, numbers, fields, dual, down):
    bins, rows, total, lanes, depth = dims
    tiles, columns = (rows + 2 * EDGE) // 8, lanes // 128
    c, me, z_base = place(dims)
    inv = [[numbers[9 + 3 * m + n] for n in range(3)] for m in range(3)]
    threshold = numbers[18]
    squared = threshold * threshold
    lane = lax.broadcasted_iota(jnp.int32, (8, 128), 1)
    sub = lax.broadcasted_iota(jnp.int32, (8, 128), 0)
    last_lane, first_lane = lane == 127, lane == 0
    last_sub, first_sub = sub == 7, sub == 0
    at_end = last_sub & (me == 3)
    zero = jnp.zeros((8, 128), jnp.float32)

    def at(t, col):
        return slice(8 * t, 8 * t + 8), slice(128 * col, 128 * col + 128)

    def layer_step(i, turn):
        src, dst, first = fields[turn], fields[turn + 1], fields[0]
        final = turn == ITERS - 1
        to = i - 2 if final else i
        z = z_base + i
        z_inside = ((z >= 0) & (z < depth - 1)).astype(jnp.float32)

        def load(ref, m, layer, t, col):
            return ref[(m, layer) + at(t, col)]

        right = [None] * tiles
        for col in range(columns):
            below = None
            f = [load(src, m, i, 0, col) for m in range(3)]
            for t in range(tiles):
                following = None
                if t + 1 < tiles:
                    following = [load(src, m, i, t + 1, col) for m in range(3)]
                v = []
                for m in range(3):
                    gz = (load(src, m, i + 1, t, col) - f[m]) * z_inside
                    up = pltpu.roll(f[m], 7, 0)
                    if following is not None:
                        up = jnp.where(last_sub, pltpu.roll(following[m], 7, 0), up)
                    else:
                        up = jnp.where(at_end, f[m], up)
                    nxt = f[m]
                    if col + 1 < columns:
                        nxt = pltpu.roll(load(src, m, i, t, col + 1), 127, 1)
                    ahead = jnp.where(last_lane, nxt, pltpu.roll(f[m], 127, 1))
                    v.append([gz, up - f[m], ahead - f[m]])
                old = None
                if turn > 0:
                    old = [[load(dual, 3 * m + d, i, t, col) for d in range(3)] for m in range(3)]
                    v = [[v[m][d] + old[m][d] for d in range(3)] for m in range(3)]
                squares = [v[m][0] * v[m][0] + v[m][1] * v[m][1] + v[m][2] * v[m][2] for m in range(3)]
                scale = threshold * lax.rsqrt(jnp.maximum(squares[0] + squares[1] + squares[2], squared))
                if final:
                    scale = scale + scale
                fresh = [[v[m][d] * scale for d in range(3)] for m in range(3)]
                if not final:
                    for m in range(3):
                        for d in range(3):
                            dual[(3 * m + d, i) + at(t, col)] = fresh[m][d]
                if turn == 0:
                    step = fresh
                elif final:
                    step = [[fresh[m][d] - old[m][d] for d in range(3)] for m in range(3)]
                else:
                    step = [[(fresh[m][d] + fresh[m][d]) - old[m][d] for d in range(3)] for m in range(3)]
                lower = [down[(m,) + at(t, col)] for m in range(3)]
                for m in range(3):
                    down[(m,) + at(t, col)] = step[m][0]
                rolled_y = [pltpu.roll(step[m][1], 1, 0) for m in range(3)]
                rolled_x = [pltpu.roll(step[m][2], 1, 1) for m in range(3)]
                rhs = []
                for m in range(3):
                    prev_y = jnp.where(first_sub, zero if below is None else below[m], rolled_y[m])
                    prev_x = jnp.where(first_lane, zero if right[t] is None else right[t][m], rolled_x[m])
                    div = (step[m][0] - lower[m]) + (step[m][1] - prev_y) + (step[m][2] - prev_x)
                    if turn == 0:
                        div = div + div
                    rhs.append(12.0 * f[m] + div)
                below, right[t] = rolled_y, rolled_x
                for m in range(3):
                    dst[(m, to) + at(t, col)] = load(first, m, i, t, col) + (
                        inv[m][0] * rhs[0] + inv[m][1] * rhs[1] + inv[m][2] * rhs[2]
                    )
                f = following

    def run(start, count, turn):
        def body(i, carry):
            layer_step(start + i, turn)
            return carry

        lax.fori_loop(0, count, body, 0)

    def correct(i, turn):
        dst = fields[turn + 1]
        to = i - 2 if turn == ITERS - 1 else i
        for col in range(columns):
            for t in range(tiles):
                low = [down[(m,) + at(t, col)] for m in range(3)]
                if turn == 0:
                    low = [e + e for e in low]
                for m in range(3):
                    dst[(m, to) + at(t, col)] = dst[(m, to) + at(t, col)] - (
                        inv[m][0] * low[0] + inv[m][1] * low[1] + inv[m][2] * low[2]
                    )

    return run, correct


def inner_kernel(dims, numbers, cross, held, f0, f1, f2, f3, dual, kept, down):
    c, me, z_base = place(dims)
    for core in range(2):

        @pl.when(c == core)
        def _(core=core):
            for k, to in enumerate(((5, 6, 9), (0, 3, 4))[core]):
                f0[:, to] = cross[:, k]

    run, correct = layer_stepper(dims, numbers, (f0, f1, f2, f3), dual, down)
    for turn in range(ITERS):
        down[...] = jnp.zeros_like(down)
        run(jnp.where(c == 0, 3, 0) + turn, 6 - 2 * turn, turn)
        kept[turn] = down[...]


def outer_kernel(dims, numbers, far, near, g0, g1, g2, g3, gd, kept, f0, f1, f2, f3, dual, o0, o1, o2, o3, down):
    bins, rows, total, lanes, depth = dims
    c, me, z_base = place(dims)
    for core in range(2):

        @pl.when(c == core)
        def _(core=core):
            for k, to in enumerate(((1, 2, 0), (7, 8, 9))[core]):
                f0[:, to] = far[:, k] if k < 2 else near[:, 0]

    run, correct = layer_stepper(dims, numbers, (f0, f1, f2, f3), dual, down)
    for turn in range(ITERS):

        @pl.when(c == 0)
        def _():
            down[...] = jnp.zeros_like(down)

        @pl.when(c == 1)
        def _(turn=turn):
            down[...] = kept[turn]

        run(jnp.where(c == 0, turn, 6 - turn), 3, turn)

        @pl.when(c == 0)
        def _(turn=turn):
            correct(3 + turn, turn)

    outs = (o0, o1, o2, o3)
    twist = twist_of(c, lax.axis_index("slab") // 2, lax.axis_size("slab"))
    for quarter in range(4):
        for turned in {0, TWIST}:

            @pl.when((me == quarter) & (twist == turned))
            def _(quarter=quarter, turned=turned):
                start = rows * quarter - window_start(quarter, rows, total)
                for j in range(4):
                    outs[ROUNDS.index(j ^ quarter ^ turned)][...] = f3[:, 1 + j, start : start + rows, :]


def twist_of(core, plane, slabs):
    return TWIST * ((core + plane // (slabs // 4)) % 2)


def gather_kernel(rows, r0, r1, r2, r3, out, sem):
    slabs = lax.axis_size("slab")
    z = lax.axis_index("bin") * slabs + lax.axis_index("slab")
    twist = twist_of(z // 4 % 2, z // 8, slabs)
    copies = []
    for n, (t, ref) in enumerate(zip(ROUNDS, (r0, r1, r2, r3))):
        at = pl.multiple_of((z % 4 ^ t ^ twist) * rows, 8)
        copies.append(pltpu.make_async_copy(ref, out.at[:, 0, pl.ds(at, rows), :], sem.at[n]))
        copies[-1].start()
    for copy in copies:
        copy.wait()


def call(kernel, outs, args, spaces=None, scratch=(), aliases=None, flops=0, out_space=VMEM):
    shapes = [jax.ShapeDtypeStruct(o, jnp.float32) for o in outs]
    spaces = spaces or [VMEM] * len(args)
    held = sum(math.prod(a.shape) for a in (*shapes, *args, *scratch))
    return pl.pallas_call(
        kernel,
        out_shape=shapes,
        in_specs=[pl.BlockSpec(memory_space=m) for m in spaces],
        out_specs=[pl.BlockSpec(memory_space=m) for m in [out_space] * len(outs)],
        scratch_shapes=list(scratch),
        input_output_aliases=aliases or {},
        cost_estimate=pl.CostEstimate(flops=flops, bytes_accessed=4 * held, transcendentals=0),
        compiler_params=pltpu.CompilerParams(vmem_limit_bytes=4 * held + (2 << 20)),
    )(*args)


def on_device(mesh_bin, mesh_slab, volumes, attenuation, penalty, tv_weight):
    own_bins, layers, total, lanes = volumes.shape
    bins = own_bins * mesh_bin
    assert mesh_bin == 4 and own_bins == 2 and layers == 4 and mesh_slab % 4 == 0
    rows = total // 4
    width = rows + 2 * EDGE
    depth = layers * mesh_slab
    devices = [(b, s) for b in range(mesh_bin) for s in range(mesh_slab)]

    def send(x, where):
        pairs = []
        for b, s in devices:
            to = where(b, s)
            if 0 <= to[0] < mesh_bin and 0 <= to[1] < mesh_slab:
                pairs.append((b * mesh_slab + s, to[0] * mesh_slab + to[1]))
        return lax.ppermute(x, ("bin", "slab"), pairs)

    dims = (bins, rows, total, lanes, depth)
    away = call(away_kernel, [(2, total, lanes)] * 2, (volumes,))
    others = [send(part, lambda b, s: (b ^ 1, s)) for part in away]
    win = (3, 2, width, lanes)
    parts = []
    for e, other in enumerate(others):
        own, to_x, to_y, to_xy = call(
            functools.partial(project_kernel, dims, e),
            [(3, width, lanes)] * 4,
            (attenuation.T, volumes, other),
            scratch=[VMEM((3, total, lanes), jnp.float32)],
        )
        from_xy = send(to_xy, lambda b, s: (b ^ 2, s ^ 1))
        from_x = send(to_x, lambda b, s: (b ^ 2, s))
        from_y = send(to_y, lambda b, s: (b, s ^ 1))
        parts += [own, from_x, from_y, from_xy]
    numbers = call(
        functools.partial(ready_kernel, bins), [(19, 8, 128)], (penalty, tv_weight, attenuation.T)
    )[0]
    state = [(3, 10, width, lanes)] * 3 + [(3, 5, width, lanes), (9, 9, width, lanes)]
    f0, far, near, cross = call(
        functools.partial(sum_kernel, dims),
        [state[0], win, (3, 1, width, lanes), (3, 3, width, lanes)],
        (numbers, *parts),
    )
    far = send(far, lambda b, s: (b ^ 1, s + (2 if b % 2 else -2)))
    near = send(near, lambda b, s: (b, s + (-2 if b % 2 else 2)))
    cross = send(cross, lambda b, s: (b ^ 1, s))
    work = 150 * width * lanes
    scratch = [VMEM((3, width, lanes), jnp.float32)]
    inner = call(
        functools.partial(inner_kernel, dims),
        state + [(3, 3, width, lanes)],
        (numbers, cross, f0),
        None,
        scratch,
        {2: 0},
        12 * work,
    )
    blocks = call(
        functools.partial(outer_kernel, dims),
        state + [(3, rows, lanes)] * 4,
        (numbers, far, near, *inner),
        None,
        scratch,
        {3 + i: i for i in range(5)},
        9 * work,
    )[5:]

    def owner(t):
        def where(b, s):
            j = t ^ (2 * (b // 2) + s % 2) ^ twist_of(b % 2, s // 2, mesh_slab)
            z = (s // 2) * 8 + 4 * (b % 2) + j
            return z // mesh_slab, z % mesh_slab

        return where

    blocks = [send(block, owner(key)) for key, block in zip(ROUNDS, blocks)]
    return call(
        functools.partial(gather_kernel, rows),
        [(3, 1, total, lanes)],
        blocks,
        scratch=[pltpu.SemaphoreType.DMA((4,))],
        out_space=pl.ANY,
    )[0]


def solution(mesh):
    placed = (P("bin", "slab", None, None), P(), P(), P())
    return jax.shard_map(
        functools.partial(on_device, mesh.shape["bin"], mesh.shape["slab"]),
        mesh=mesh,
        in_specs=placed,
        out_specs=P(None, ("bin", "slab"), None, None),
        check_vma=False,
    )
```

```python
import functools
import math

import jax
import jax.numpy as jnp
from jax import lax
from jax.experimental import pallas as pl
from jax.experimental.pallas import tpu as pltpu
from jax.sharding import PartitionSpec as P

ITERS = 3
EDGE = 4
ROUNDS = (1, 3, 0, 2)
TWISTS = 0
VMEM = pltpu.VMEM


def window_start(quarter, rows, total):
    return min(max(rows * quarter - EDGE, 0), total - rows - 2 * EDGE)


def inverse_three(m):
    cof = [
        [
            m[(r + 1) % 3][(c + 1) % 3] * m[(r + 2) % 3][(c + 2) % 3]
            - m[(r + 1) % 3][(c + 2) % 3] * m[(r + 2) % 3][(c + 1) % 3]
            for c in range(3)
        ]
        for r in range(3)
    ]
    det = m[0][0] * cof[0][0] + m[0][1] * cof[0][1] + m[0][2] * cof[0][2]
    over = 1.0 / det
    return [[cof[c][r] * over for c in range(3)] for r in range(3)]


def away_kernel(volumes, first, second):
    c = lax.axis_index("bin") % 2
    for e, ref in enumerate((first, second)):
        for k in range(2):
            ref[k] = volumes[k, 2 * (1 - c) + e]


def spread(x):
    return jnp.broadcast_to(x, (8, 128))


def ready_kernel(bins, pen, tvw, att, numbers):
    a = [[att[bins * m + k] for k in range(bins)] for m in range(3)]
    pen_value = spread(pen[...].reshape(1, 1))
    gram = [[None] * 3 for _ in range(3)]
    for i in range(3):
        for j in range(i, 3):
            total = a[i][0] * a[j][0]
            for k in range(1, bins):
                total = total + a[i][k] * a[j][k]
            gram[i][j] = gram[j][i] = total
    for i in range(3):
        gram[i][i] = gram[i][i] + 12.0 * pen_value
    inv = inverse_three(gram)
    for m in range(3):
        for n in range(3):
            numbers[3 * m + n] = inv[m][n]
            numbers[9 + 3 * m + n] = pen_value * inv[m][n]
    numbers[18] = spread(tvw[...].reshape(1, 1)) / pen_value


def project_kernel(dims, e, att, volumes, other, own, to_x, to_y, to_xy, part):
    bins, rows, total, lanes, depth = dims
    c, me, z_base = place(dims)
    b = lax.axis_index("bin")
    a = [[att[bins * m + k] for k in range(bins)] for m in range(3)]
    w = []
    for k in range(4):
        group = b if k < 2 else b ^ 1
        row = []
        for m in range(3):
            value = a[m][k % 2]
            for g in range(1, bins // 2):
                value = jnp.where(group == g, a[m][2 * g + k % 2], value)
            row.append(value)
        w.append(row)

    def body(t, carry):
        tile = pl.ds(pl.multiple_of(t * 8, 8), 8)
        for col in range(lanes // 128):
            at = (tile, slice(128 * col, 128 * col + 128))
            v = [volumes[(0, 2 * c + e, *at)], volumes[(1, 2 * c + e, *at)], other[(0, *at)], other[(1, *at)]]
            for m in range(3):
                part[(m, *at)] = v[0] * w[0][m] + v[1] * w[1][m] + (v[2] * w[2][m] + v[3] * w[3][m])
        return carry

    lax.fori_loop(0, total // 8, body, 0)
    width = rows + 2 * EDGE
    for rel, ref in enumerate((own, to_y, to_x, to_xy)):
        for quarter in range(4):

            @pl.when((me ^ rel) == quarter)
            def _(ref=ref, quarter=quarter):
                start = window_start(quarter, rows, total)
                ref[...] = part[:, start : start + width, :]


def sum_kernel(dims, numbers, *refs):
    parts, (f0, far, near, cross) = (refs[:4], refs[4:8]), refs[8:]
    y = lax.axis_index("slab") % 2
    c = lax.axis_index("bin") % 2
    bins, rows, total, lanes, depth = dims
    inv = [[numbers[3 * m + n] for n in range(3)] for m in range(3)]
    for e in range(2):
        own, from_x, from_y, from_xy = parts[e]
        for to, one, two in ((3 + 4 * y, own, from_x), (7 - 4 * y, from_y, from_xy)):
            for t in range((rows + 2 * EDGE) // 8):
                for col in range(lanes // 128):
                    at = (slice(8 * t, 8 * t + 8), slice(128 * col, 128 * col + 128))
                    d = [one[(m, *at)] + two[(m, *at)] for m in range(3)]
                    for m in range(3):
                        f0[(m, to - 2 * c + e, *at)] = inv[m][0] * d[0] + inv[m][1] * d[1] + inv[m][2] * d[2]
    for core in range(2):

        @pl.when(c == core)
        def _(core=core):
            slab = [f0.at[:, 3 + 4 * k - 2 * core + e] for k in range(2) for e in range(2)]
            far[:, 0] = slab[2 * core][...]
            far[:, 1] = slab[2 * core + 1][...]
            near[:, 0] = slab[2 * (1 - core) + 1 - core][...]
            for at, k in enumerate(((1, 2, 3), (0, 1, 2))[core]):
                cross[:, at] = slab[k][...]


def place(dims):
    bins, rows, total, lanes, depth = dims
    b = lax.axis_index("bin")
    s = lax.axis_index("slab")
    c = b % 2
    return c, 2 * (b // 2) + s % 2, (s // 2) * 8 + 4 * c - 3


def layer_stepper(dims, numbers, fields, dual, down):
    bins, rows, total, lanes, depth = dims
    tiles, columns = (rows + 2 * EDGE) // 8, lanes // 128
    c, me, z_base = place(dims)
    inv = [[numbers[9 + 3 * m + n] for n in range(3)] for m in range(3)]
    threshold = numbers[18]
    squared = threshold * threshold
    lane = lax.broadcasted_iota(jnp.int32, (8, 128), 1)
    sub = lax.broadcasted_iota(jnp.int32, (8, 128), 0)
    last_lane, first_lane = lane == 127, lane == 0
    last_sub, first_sub = sub == 7, sub == 0
    at_end = last_sub & (me == 3)
    zero = jnp.zeros((8, 128), jnp.float32)

    def at(t, col):
        return slice(8 * t, 8 * t + 8), slice(128 * col, 128 * col + 128)

    def layer_step(i, turn):
        src, dst, first = fields[turn], fields[turn + 1], fields[0]
        final = turn == ITERS - 1
        to = i - 2 if final else i
        z = z_base + i
        z_inside = ((z >= 0) & (z < depth - 1)).astype(jnp.float32)

        def load(ref, m, layer, t, col):
            return ref[(m, layer) + at(t, col)]

        right = [None] * tiles
        for col in range(columns):
            below = None
            f = [load(src, m, i, 0, col) for m in range(3)]
            for t in range(tiles):
                following = None
                if t + 1 < tiles:
                    following = [load(src, m, i, t + 1, col) for m in range(3)]
                v = []
                for m in range(3):
                    gz = (load(src, m, i + 1, t, col) - f[m]) * z_inside
                    up = pltpu.roll(f[m], 7, 0)
                    if following is not None:
                        up = jnp.where(last_sub, pltpu.roll(following[m], 7, 0), up)
                    else:
                        up = jnp.where(at_end, f[m], up)
                    nxt = f[m]
                    if col + 1 < columns:
                        nxt = pltpu.roll(load(src, m, i, t, col + 1), 127, 1)
                    ahead = jnp.where(last_lane, nxt, pltpu.roll(f[m], 127, 1))
                    v.append([gz, up - f[m], ahead - f[m]])
                old = None
                if turn > 0:
                    old = [[load(dual, 3 * m + d, i, t, col) for d in range(3)] for m in range(3)]
                    v = [[v[m][d] + old[m][d] for d in range(3)] for m in range(3)]
                squares = [v[m][0] * v[m][0] + v[m][1] * v[m][1] + v[m][2] * v[m][2] for m in range(3)]
                scale = threshold * lax.rsqrt(jnp.maximum(squares[0] + squares[1] + squares[2], squared))
                if final:
                    scale = scale + scale
                fresh = [[v[m][d] * scale for d in range(3)] for m in range(3)]
                if not final:
                    for m in range(3):
                        for d in range(3):
                            dual[(3 * m + d, i) + at(t, col)] = fresh[m][d]
                if turn == 0:
                    step = fresh
                elif final:
                    step = [[fresh[m][d] - old[m][d] for d in range(3)] for m in range(3)]
                else:
                    step = [[(fresh[m][d] + fresh[m][d]) - old[m][d] for d in range(3)] for m in range(3)]
                lower = [down[(m,) + at(t, col)] for m in range(3)]
                for m in range(3):
                    down[(m,) + at(t, col)] = step[m][0]
                rolled_y = [pltpu.roll(step[m][1], 1, 0) for m in range(3)]
                rolled_x = [pltpu.roll(step[m][2], 1, 1) for m in range(3)]
                rhs = []
                for m in range(3):
                    prev_y = jnp.where(first_sub, zero if below is None else below[m], rolled_y[m])
                    prev_x = jnp.where(first_lane, zero if right[t] is None else right[t][m], rolled_x[m])
                    div = (step[m][0] - lower[m]) + (step[m][1] - prev_y) + (step[m][2] - prev_x)
                    if turn == 0:
                        div = div + div
                    rhs.append(12.0 * f[m] + div)
                below, right[t] = rolled_y, rolled_x
                for m in range(3):
                    dst[(m, to) + at(t, col)] = load(first, m, i, t, col) + (
                        inv[m][0] * rhs[0] + inv[m][1] * rhs[1] + inv[m][2] * rhs[2]
                    )
                f = following

    def run(start, count, turn):
        def body(i, carry):
            layer_step(start + i, turn)
            return carry

        lax.fori_loop(0, count, body, 0)

    def correct(i, turn):
        dst = fields[turn + 1]
        to = i - 2 if turn == ITERS - 1 else i
        for col in range(columns):
            for t in range(tiles):
                low = [down[(m,) + at(t, col)] for m in range(3)]
                if turn == 0:
                    low = [e + e for e in low]
                for m in range(3):
                    dst[(m, to) + at(t, col)] = dst[(m, to) + at(t, col)] - (
                        inv[m][0] * low[0] + inv[m][1] * low[1] + inv[m][2] * low[2]
                    )

    return run, correct


def inner_kernel(dims, numbers, cross, held, f0, f1, f2, f3, dual, kept, down):
    c, me, z_base = place(dims)
    for core in range(2):

        @pl.when(c == core)
        def _(core=core):
            for k, to in enumerate(((5, 6, 9), (0, 3, 4))[core]):
                f0[:, to] = cross[:, k]

    run, correct = layer_stepper(dims, numbers, (f0, f1, f2, f3), dual, down)
    for turn in range(ITERS):
        down[...] = jnp.zeros_like(down)
        run(jnp.where(c == 0, 3, 0) + turn, 6 - 2 * turn, turn)
        kept[turn] = down[...]


def outer_kernel(dims, numbers, far, near, g0, g1, g2, g3, gd, kept, f0, f1, f2, f3, dual, o0, o1, o2, o3, down):
    bins, rows, total, lanes, depth = dims
    c, me, z_base = place(dims)
    for core in range(2):

        @pl.when(c == core)
        def _(core=core):
            for k, to in enumerate(((1, 2, 0), (7, 8, 9))[core]):
                f0[:, to] = far[:, k] if k < 2 else near[:, 0]

    run, correct = layer_stepper(dims, numbers, (f0, f1, f2, f3), dual, down)
    for turn in range(ITERS):

        @pl.when(c == 0)
        def _():
            down[...] = jnp.zeros_like(down)

        @pl.when(c == 1)
        def _(turn=turn):
            down[...] = kept[turn]

        run(jnp.where(c == 0, turn, 6 - turn), 3, turn)

        @pl.when(c == 0)
        def _(turn=turn):
            correct(3 + turn, turn)

    twist = twist_of(c, lax.axis_index("slab") // 2, lax.axis_size("slab"))
    for quarter in range(4):

        @pl.when(me == quarter)
        def _(quarter=quarter):
            start = rows * quarter - window_start(quarter, rows, total)
            for key, out in zip(ROUNDS, (o0, o1, o2, o3)):
                out[...] = f3[:, 1 + (key ^ quarter ^ twist), start : start + rows, :]


def twist_of(core, plane, slabs):
    return (TWISTS >> (2 * (4 * core + plane // (slabs // 8)))) & 3


def gather_kernel(rows, r0, r1, r2, r3, out, sem):
    slabs = lax.axis_size("slab")
    z = lax.axis_index("bin") * slabs + lax.axis_index("slab")
    twist = twist_of(z // 4 % 2, z // 8, slabs)
    copies = []
    for n, (t, ref) in enumerate(zip(ROUNDS, (r0, r1, r2, r3))):
        at = pl.multiple_of((z % 4 ^ t ^ twist) * rows, 8)
        copies.append(pltpu.make_async_copy(ref, out.at[:, 0, pl.ds(at, rows), :], sem.at[n]))
        copies[-1].start()
    for copy in copies:
        copy.wait()


def call(kernel, outs, args, spaces=None, scratch=(), aliases=None, flops=0, out_space=VMEM):
    shapes = [jax.ShapeDtypeStruct(o, jnp.float32) for o in outs]
    spaces = spaces or [VMEM] * len(args)
    held = sum(math.prod(a.shape) for a in (*shapes, *args, *scratch))
    return pl.pallas_call(
        kernel,
        out_shape=shapes,
        in_specs=[pl.BlockSpec(memory_space=m) for m in spaces],
        out_specs=[pl.BlockSpec(memory_space=m) for m in [out_space] * len(outs)],
        scratch_shapes=list(scratch),
        input_output_aliases=aliases or {},
        cost_estimate=pl.CostEstimate(flops=flops, bytes_accessed=4 * held, transcendentals=0),
        compiler_params=pltpu.CompilerParams(vmem_limit_bytes=4 * held + (2 << 20)),
    )(*args)


def on_device(mesh_bin, mesh_slab, volumes, attenuation, penalty, tv_weight):
    own_bins, layers, total, lanes = volumes.shape
    bins = own_bins * mesh_bin
    assert mesh_bin == 4 and own_bins == 2 and layers == 4 and mesh_slab % 4 == 0
    rows = total // 4
    width = rows + 2 * EDGE
    depth = layers * mesh_slab
    devices = [(b, s) for b in range(mesh_bin) for s in range(mesh_slab)]

    def send(x, where):
        pairs = []
        for b, s in devices:
            to = where(b, s)
            if 0 <= to[0] < mesh_bin and 0 <= to[1] < mesh_slab:
                pairs.append((b * mesh_slab + s, to[0] * mesh_slab + to[1]))
        return lax.ppermute(x, ("bin", "slab"), pairs)

    dims = (bins, rows, total, lanes, depth)
    spreads = jnp.broadcast_to(attenuation.T.reshape(3 * bins, 1, 1), (3 * bins, 8, 128))
    away = call(away_kernel, [(2, total, lanes)] * 2, (volumes,))
    others = [send(part, lambda b, s: (b ^ 1, s)) for part in away]
    win = (3, 2, width, lanes)
    parts = []
    for e, other in enumerate(others):
        own, to_x, to_y, to_xy = call(
            functools.partial(project_kernel, dims, e),
            [(3, width, lanes)] * 4,
            (spreads, volumes, other),
            scratch=[VMEM((3, total, lanes), jnp.float32)],
        )
        from_xy = send(to_xy, lambda b, s: (b ^ 2, s ^ 1))
        from_x = send(to_x, lambda b, s: (b ^ 2, s))
        from_y = send(to_y, lambda b, s: (b, s ^ 1))
        parts += [own, from_x, from_y, from_xy]
    numbers = call(
        functools.partial(ready_kernel, bins), [(19, 8, 128)], (penalty, tv_weight, spreads)
    )[0]
    state = [(3, 10, width, lanes)] * 3 + [(3, 5, width, lanes), (9, 9, width, lanes)]
    f0, far, near, cross = call(
        functools.partial(sum_kernel, dims),
        [state[0], win, (3, 1, width, lanes), (3, 3, width, lanes)],
        (numbers, *parts),
    )
    far = send(far, lambda b, s: (b ^ 1, s + (2 if b % 2 else -2)))
    near = send(near, lambda b, s: (b, s + (-2 if b % 2 else 2)))
    cross = send(cross, lambda b, s: (b ^ 1, s))
    work = 150 * width * lanes
    scratch = [VMEM((3, width, lanes), jnp.float32)]
    inner = call(
        functools.partial(inner_kernel, dims),
        state + [(3, 3, width, lanes)],
        (numbers, cross, f0),
        None,
        scratch,
        {2: 0},
        12 * work,
    )
    blocks = call(
        functools.partial(outer_kernel, dims),
        state + [(3, rows, lanes)] * 4,
        (numbers, far, near, *inner),
        None,
        scratch,
        {3 + i: i for i in range(5)},
        9 * work,
    )[5:]

    def owner(t):
        def where(b, s):
            j = t ^ (2 * (b // 2) + s % 2) ^ twist_of(b % 2, s // 2, mesh_slab)
            z = (s // 2) * 8 + 4 * (b % 2) + j
            return z // mesh_slab, z % mesh_slab

        return where

    blocks = [send(block, owner(key)) for key, block in zip(ROUNDS, blocks)]
    return call(
        functools.partial(gather_kernel, rows),
        [(3, 1, total, lanes)],
        blocks,
        scratch=[pltpu.SemaphoreType.DMA((4,))],
        out_space=pl.ANY,
    )[0]


def solution(mesh):
    placed = (P("bin", "slab", None, None), P(), P(), P())
    return jax.shard_map(
        functools.partial(on_device, mesh.shape["bin"], mesh.shape["slab"]),
        mesh=mesh,
        in_specs=placed,
        out_specs=P(None, ("bin", "slab"), None, None),
        check_vma=False,
    )
```

```python
import functools
import math

import jax
import jax.numpy as jnp
from jax import lax
from jax.experimental import pallas as pl
from jax.experimental.pallas import tpu as pltpu
from jax.sharding import PartitionSpec as P

ITERS = 3
EDGE = 4
GRANT = 56_000 * 1024
ROUNDS = (1, 3, 0, 2)
TWISTS = 0
VMEM = pltpu.VMEM


def window_start(quarter, rows, total):
    return min(max(rows * quarter - EDGE, 0), total - rows - 2 * EDGE)


def inverse_three(m):
    cof = [
        [
            m[(r + 1) % 3][(c + 1) % 3] * m[(r + 2) % 3][(c + 2) % 3]
            - m[(r + 1) % 3][(c + 2) % 3] * m[(r + 2) % 3][(c + 1) % 3]
            for c in range(3)
        ]
        for r in range(3)
    ]
    det = m[0][0] * cof[0][0] + m[0][1] * cof[0][1] + m[0][2] * cof[0][2]
    over = 1.0 / det
    return [[cof[c][r] * over for c in range(3)] for r in range(3)]


def away_kernel(volumes, first, second, sem):
    c = lax.axis_index("bin") % 2
    copies = [
        pltpu.make_async_copy(volumes.at[k, 2 * (1 - c) + e], ref.at[k], sem.at[e, k])
        for e, ref in enumerate((first, second))
        for k in range(2)
    ]
    for copy in copies:
        copy.start()
    for copy in copies:
        copy.wait()


def spread(x):
    return jnp.broadcast_to(x, (8, 128))


def ready_kernel(bins, pen, tvw, att, numbers):
    a = [[att[bins * m + k] for k in range(bins)] for m in range(3)]
    pen_value = spread(pen[...].reshape(1, 1))
    gram = [[None] * 3 for _ in range(3)]
    for i in range(3):
        for j in range(i, 3):
            total = a[i][0] * a[j][0]
            for k in range(1, bins):
                total = total + a[i][k] * a[j][k]
            gram[i][j] = gram[j][i] = total
    for i in range(3):
        gram[i][i] = gram[i][i] + 12.0 * pen_value
    inv = inverse_three(gram)
    for m in range(3):
        for n in range(3):
            numbers[3 * m + n] = inv[m][n]
            numbers[9 + 3 * m + n] = pen_value * inv[m][n]
    numbers[18] = spread(tvw[...].reshape(1, 1)) / pen_value


def project_kernel(dims, e, att, volumes, other, own, to_x, to_y, to_xy, part):
    bins, rows, total, lanes, depth = dims
    c, me, z_base = place(dims)
    b = lax.axis_index("bin")
    a = [[att[bins * m + k] for k in range(bins)] for m in range(3)]
    w = []
    for k in range(4):
        group = b if k < 2 else b ^ 1
        row = []
        for m in range(3):
            value = a[m][k % 2]
            for g in range(1, bins // 2):
                value = jnp.where(group == g, a[m][2 * g + k % 2], value)
            row.append(value)
        w.append(row)

    def body(t, carry):
        tile = pl.ds(pl.multiple_of(t * 8, 8), 8)
        for col in range(lanes // 128):
            at = (tile, slice(128 * col, 128 * col + 128))
            v = [volumes[(0, 2 * c + e, *at)], volumes[(1, 2 * c + e, *at)], other[(0, *at)], other[(1, *at)]]
            for m in range(3):
                part[(m, *at)] = v[0] * w[0][m] + v[1] * w[1][m] + (v[2] * w[2][m] + v[3] * w[3][m])
        return carry

    lax.fori_loop(0, total // 8, body, 0)
    width = rows + 2 * EDGE
    for rel, ref in enumerate((own, to_y, to_x, to_xy)):
        for quarter in range(4):

            @pl.when((me ^ rel) == quarter)
            def _(ref=ref, quarter=quarter):
                start = window_start(quarter, rows, total)
                ref[...] = part[:, start : start + width, :]


def sum_kernel(dims, numbers, *refs):
    parts, (f0, far, near, cross) = (refs[:4], refs[4:8]), refs[8:]
    y = lax.axis_index("slab") % 2
    c = lax.axis_index("bin") % 2
    bins, rows, total, lanes, depth = dims
    inv = [[numbers[3 * m + n] for n in range(3)] for m in range(3)]
    for e in range(2):
        own, from_x, from_y, from_xy = parts[e]
        for to, one, two in ((3 + 4 * y, own, from_x), (7 - 4 * y, from_y, from_xy)):
            for t in range((rows + 2 * EDGE) // 8):
                for col in range(lanes // 128):
                    at = (slice(8 * t, 8 * t + 8), slice(128 * col, 128 * col + 128))
                    d = [one[(m, *at)] + two[(m, *at)] for m in range(3)]
                    for m in range(3):
                        f0[(m, to - 2 * c + e, *at)] = inv[m][0] * d[0] + inv[m][1] * d[1] + inv[m][2] * d[2]
    for core in range(2):

        @pl.when(c == core)
        def _(core=core):
            slab = [f0.at[:, 3 + 4 * k - 2 * core + e] for k in range(2) for e in range(2)]
            far[:, 0] = slab[2 * core][...]
            far[:, 1] = slab[2 * core + 1][...]
            near[:, 0] = slab[2 * (1 - core) + 1 - core][...]
            for at, k in enumerate(((1, 2, 3), (0, 1, 2))[core]):
                cross[:, at] = slab[k][...]


def place(dims):
    bins, rows, total, lanes, depth = dims
    b = lax.axis_index("bin")
    s = lax.axis_index("slab")
    c = b % 2
    return c, 2 * (b // 2) + s % 2, (s // 2) * 8 + 4 * c - 3


def layer_stepper(dims, numbers, fields, dual, down):
    bins, rows, total, lanes, depth = dims
    tiles, columns = (rows + 2 * EDGE) // 8, lanes // 128
    c, me, z_base = place(dims)
    inv = [[numbers[9 + 3 * m + n] for n in range(3)] for m in range(3)]
    threshold = numbers[18]
    squared = threshold * threshold
    lane = lax.broadcasted_iota(jnp.int32, (8, 128), 1)
    sub = lax.broadcasted_iota(jnp.int32, (8, 128), 0)
    last_lane, first_lane = lane == 127, lane == 0
    last_sub, first_sub = sub == 7, sub == 0
    at_end = last_sub & (me == 3)
    zero = jnp.zeros((8, 128), jnp.float32)

    def at(t, col):
        return slice(8 * t, 8 * t + 8), slice(128 * col, 128 * col + 128)

    def layer_step(i, turn):
        src, dst, first = fields[turn], fields[turn + 1], fields[0]
        final = turn == ITERS - 1
        to = i - 2 if final else i
        z = z_base + i
        z_inside = ((z >= 0) & (z < depth - 1)).astype(jnp.float32)

        def load(ref, m, layer, t, col):
            return ref[(m, layer) + at(t, col)]

        right = [None] * tiles
        for col in range(columns):
            below = None
            f = [load(src, m, i, 0, col) for m in range(3)]
            for t in range(tiles):
                following = None
                if t + 1 < tiles:
                    following = [load(src, m, i, t + 1, col) for m in range(3)]
                v = []
                for m in range(3):
                    gz = (load(src, m, i + 1, t, col) - f[m]) * z_inside
                    up = pltpu.roll(f[m], 7, 0)
                    if following is not None:
                        up = jnp.where(last_sub, pltpu.roll(following[m], 7, 0), up)
                    else:
                        up = jnp.where(at_end, f[m], up)
                    nxt = f[m]
                    if col + 1 < columns:
                        nxt = pltpu.roll(load(src, m, i, t, col + 1), 127, 1)
                    ahead = jnp.where(last_lane, nxt, pltpu.roll(f[m], 127, 1))
                    v.append([gz, up - f[m], ahead - f[m]])
                old = None
                if turn > 0:
                    old = [[load(dual, 3 * m + d, i, t, col) for d in range(3)] for m in range(3)]
                    v = [[v[m][d] + old[m][d] for d in range(3)] for m in range(3)]
                squares = [v[m][0] * v[m][0] + v[m][1] * v[m][1] + v[m][2] * v[m][2] for m in range(3)]
                scale = threshold * lax.rsqrt(jnp.maximum(squares[0] + squares[1] + squares[2], squared))
                if final:
                    scale = scale + scale
                fresh = [[v[m][d] * scale for d in range(3)] for m in range(3)]
                if not final:
                    for m in range(3):
                        for d in range(3):
                            dual[(3 * m + d, i) + at(t, col)] = fresh[m][d]
                if turn == 0:
                    step = fresh
                elif final:
                    step = [[fresh[m][d] - old[m][d] for d in range(3)] for m in range(3)]
                else:
                    step = [[(fresh[m][d] + fresh[m][d]) - old[m][d] for d in range(3)] for m in range(3)]
                lower = [down[(m,) + at(t, col)] for m in range(3)]
                for m in range(3):
                    down[(m,) + at(t, col)] = step[m][0]
                rolled_y = [pltpu.roll(step[m][1], 1, 0) for m in range(3)]
                rolled_x = [pltpu.roll(step[m][2], 1, 1) for m in range(3)]
                rhs = []
                for m in range(3):
                    prev_y = jnp.where(first_sub, zero if below is None else below[m], rolled_y[m])
                    prev_x = jnp.where(first_lane, zero if right[t] is None else right[t][m], rolled_x[m])
                    div = (step[m][0] - lower[m]) + (step[m][1] - prev_y) + (step[m][2] - prev_x)
                    if turn == 0:
                        div = div + div
                    rhs.append(12.0 * f[m] + div)
                below, right[t] = rolled_y, rolled_x
                for m in range(3):
                    dst[(m, to) + at(t, col)] = load(first, m, i, t, col) + (
                        inv[m][0] * rhs[0] + inv[m][1] * rhs[1] + inv[m][2] * rhs[2]
                    )
                f = following

    def run(start, count, turn):
        def body(i, carry):
            layer_step(start + i, turn)
            return carry

        lax.fori_loop(0, count, body, 0)

    def correct(i, turn):
        dst = fields[turn + 1]
        to = i - 2 if turn == ITERS - 1 else i
        for col in range(columns):
            for t in range(tiles):
                low = [down[(m,) + at(t, col)] for m in range(3)]
                if turn == 0:
                    low = [e + e for e in low]
                for m in range(3):
                    dst[(m, to) + at(t, col)] = dst[(m, to) + at(t, col)] - (
                        inv[m][0] * low[0] + inv[m][1] * low[1] + inv[m][2] * low[2]
                    )

    return run, correct


def inner_kernel(dims, numbers, cross, held, f0, f1, f2, f3, dual, kept, down):
    c, me, z_base = place(dims)
    for core in range(2):

        @pl.when(c == core)
        def _(core=core):
            for k, to in enumerate(((5, 6, 9), (0, 3, 4))[core]):
                f0[:, to] = cross[:, k]

    run, correct = layer_stepper(dims, numbers, (f0, f1, f2, f3), dual, down)
    for turn in range(ITERS):
        down[...] = jnp.zeros_like(down)
        run(jnp.where(c == 0, 3, 0) + turn, 6 - 2 * turn, turn)
        kept[turn] = down[...]


def outer_kernel(dims, numbers, far, near, g0, g1, g2, g3, gd, kept, f0, f1, f2, f3, dual, o0, o1, o2, o3, down):
    bins, rows, total, lanes, depth = dims
    c, me, z_base = place(dims)
    for core in range(2):

        @pl.when(c == core)
        def _(core=core):
            for k, to in enumerate(((1, 2, 0), (7, 8, 9))[core]):
                f0[:, to] = far[:, k] if k < 2 else near[:, 0]

    run, correct = layer_stepper(dims, numbers, (f0, f1, f2, f3), dual, down)
    for turn in range(ITERS):

        @pl.when(c == 0)
        def _():
            down[...] = jnp.zeros_like(down)

        @pl.when(c == 1)
        def _(turn=turn):
            down[...] = kept[turn]

        run(jnp.where(c == 0, turn, 6 - turn), 3, turn)

        @pl.when(c == 0)
        def _(turn=turn):
            correct(3 + turn, turn)

    twist = twist_of(c, lax.axis_index("slab") // 2, lax.axis_size("slab"))
    for quarter in range(4):

        @pl.when(me == quarter)
        def _(quarter=quarter):
            start = rows * quarter - window_start(quarter, rows, total)
            for key, out in zip(ROUNDS, (o0, o1, o2, o3)):
                out[...] = f3[:, 1 + (key ^ quarter ^ twist), start : start + rows, :]


def twist_of(core, plane, slabs):
    return (TWISTS >> (2 * (4 * core + plane // (slabs // 8)))) & 3


def gather_kernel(rows, r0, r1, r2, r3, out, sem):
    slabs = lax.axis_size("slab")
    z = lax.axis_index("bin") * slabs + lax.axis_index("slab")
    twist = twist_of(z // 4 % 2, z // 8, slabs)
    copies = []
    for n, (t, ref) in enumerate(zip(ROUNDS, (r0, r1, r2, r3))):
        at = pl.multiple_of((z % 4 ^ t ^ twist) * rows, 8)
        copies.append(pltpu.make_async_copy(ref, out.at[:, 0, pl.ds(at, rows), :], sem.at[n]))
        copies[-1].start()
    for copy in copies:
        copy.wait()


def call(kernel, outs, args, spaces=None, scratch=(), aliases=None, flops=0, out_space=VMEM, limit=None):
    shapes = [jax.ShapeDtypeStruct(o, jnp.float32) for o in outs]
    spaces = spaces or [VMEM] * len(args)
    held = sum(math.prod(a.shape) for a in (*shapes, *args, *scratch))
    return pl.pallas_call(
        kernel,
        out_shape=shapes,
        in_specs=[pl.BlockSpec(memory_space=m) for m in spaces],
        out_specs=[pl.BlockSpec(memory_space=m) for m in [out_space] * len(outs)],
        scratch_shapes=list(scratch),
        input_output_aliases=aliases or {},
        cost_estimate=pl.CostEstimate(flops=flops, bytes_accessed=4 * held, transcendentals=0),
        compiler_params=pltpu.CompilerParams(vmem_limit_bytes=limit or 4 * held + (2 << 20)),
    )(*args)


def on_device(mesh_bin, mesh_slab, volumes, attenuation, penalty, tv_weight):
    own_bins, layers, total, lanes = volumes.shape
    bins = own_bins * mesh_bin
    assert mesh_bin == 4 and own_bins == 2 and layers == 4 and mesh_slab % 4 == 0
    rows = total // 4
    width = rows + 2 * EDGE
    depth = layers * mesh_slab
    devices = [(b, s) for b in range(mesh_bin) for s in range(mesh_slab)]

    def send(x, where):
        pairs = []
        for b, s in devices:
            to = where(b, s)
            if 0 <= to[0] < mesh_bin and 0 <= to[1] < mesh_slab:
                pairs.append((b * mesh_slab + s, to[0] * mesh_slab + to[1]))
        return lax.ppermute(x, ("bin", "slab"), pairs)

    dims = (bins, rows, total, lanes, depth)
    spreads = jnp.broadcast_to(attenuation.T.reshape(3 * bins, 1, 1), (3 * bins, 8, 128))
    away = call(
        away_kernel,
        [(2, total, lanes)] * 2,
        (volumes,),
        [pl.ANY],
        [pltpu.SemaphoreType.DMA((2, 2))],
        limit=GRANT - 6 * 2 * total * lanes * 4,
    )
    others = [send(part, lambda b, s: (b ^ 1, s)) for part in away]
    win = (3, 2, width, lanes)
    parts = []
    for e, other in enumerate(others):
        own, to_x, to_y, to_xy = call(
            functools.partial(project_kernel, dims, e),
            [(3, width, lanes)] * 4,
            (spreads, volumes, other),
            scratch=[VMEM((3, total, lanes), jnp.float32)],
        )
        from_xy = send(to_xy, lambda b, s: (b ^ 2, s ^ 1))
        from_x = send(to_x, lambda b, s: (b ^ 2, s))
        from_y = send(to_y, lambda b, s: (b, s ^ 1))
        parts += [own, from_x, from_y, from_xy]
    numbers = call(
        functools.partial(ready_kernel, bins), [(19, 8, 128)], (penalty, tv_weight, spreads)
    )[0]
    state = [(3, 10, width, lanes)] * 3 + [(3, 5, width, lanes), (9, 9, width, lanes)]
    f0, far, near, cross = call(
        functools.partial(sum_kernel, dims),
        [state[0], win, (3, 1, width, lanes), (3, 3, width, lanes)],
        (numbers, *parts),
    )
    far = send(far, lambda b, s: (b ^ 1, s + (2 if b % 2 else -2)))
    near = send(near, lambda b, s: (b, s + (-2 if b % 2 else 2)))
    cross = send(cross, lambda b, s: (b ^ 1, s))
    work = 150 * width * lanes
    scratch = [VMEM((3, width, lanes), jnp.float32)]
    inner = call(
        functools.partial(inner_kernel, dims),
        state + [(3, 3, width, lanes)],
        (numbers, cross, f0),
        None,
        scratch,
        {2: 0},
        12 * work,
    )
    blocks = call(
        functools.partial(outer_kernel, dims),
        state + [(3, rows, lanes)] * 4,
        (numbers, far, near, *inner),
        None,
        scratch,
        {3 + i: i for i in range(5)},
        9 * work,
    )[5:]

    def owner(t):
        def where(b, s):
            j = t ^ (2 * (b // 2) + s % 2) ^ twist_of(b % 2, s // 2, mesh_slab)
            z = (s // 2) * 8 + 4 * (b % 2) + j
            return z // mesh_slab, z % mesh_slab

        return where

    blocks = [send(block, owner(key)) for key, block in zip(ROUNDS, blocks)]
    return call(
        functools.partial(gather_kernel, rows),
        [(3, 1, total, lanes)],
        blocks,
        scratch=[pltpu.SemaphoreType.DMA((4,))],
        out_space=pl.ANY,
    )[0]


def solution(mesh):
    placed = (P("bin", "slab", None, None), P(), P(), P())
    return jax.shard_map(
        functools.partial(on_device, mesh.shape["bin"], mesh.shape["slab"]),
        mesh=mesh,
        in_specs=placed,
        out_specs=P(None, ("bin", "slab"), None, None),
        check_vma=False,
    )
```

```python
import functools
import math

import jax
import jax.numpy as jnp
from jax import lax
from jax.experimental import pallas as pl
from jax.experimental.pallas import tpu as pltpu
from jax.sharding import PartitionSpec as P

ITERS = 3
EDGE = 4
GRANT = 56_000 * 1024
ROUNDS = (1, 3, 0, 2)
TWISTS = 0
VMEM = pltpu.VMEM


def window_start(quarter, rows, total):
    return min(max(rows * quarter - EDGE, 0), total - rows - 2 * EDGE)


def inverse_three(m):
    cof = [
        [
            m[(r + 1) % 3][(c + 1) % 3] * m[(r + 2) % 3][(c + 2) % 3]
            - m[(r + 1) % 3][(c + 2) % 3] * m[(r + 2) % 3][(c + 1) % 3]
            for c in range(3)
        ]
        for r in range(3)
    ]
    det = m[0][0] * cof[0][0] + m[0][1] * cof[0][1] + m[0][2] * cof[0][2]
    over = 1.0 / det
    return [[cof[c][r] * over for c in range(3)] for r in range(3)]


def away_kernel(volumes, first, second, sem):
    c = lax.axis_index("bin") % 2
    copies = [
        pltpu.make_async_copy(volumes.at[k, 2 * (1 - c) + e], ref.at[k], sem.at[e, k])
        for e, ref in enumerate((first, second))
        for k in range(2)
    ]
    for copy in copies:
        copy.start()
    for copy in copies:
        copy.wait()


def spread(x):
    return jnp.broadcast_to(x, (8, 128))


def ready_kernel(bins, pen, tvw, att, numbers):
    a = [[att[bins * m + k] for k in range(bins)] for m in range(3)]
    pen_value = spread(pen[...].reshape(1, 1))
    gram = [[None] * 3 for _ in range(3)]
    for i in range(3):
        for j in range(i, 3):
            total = a[i][0] * a[j][0]
            for k in range(1, bins):
                total = total + a[i][k] * a[j][k]
            gram[i][j] = gram[j][i] = total
    for i in range(3):
        gram[i][i] = gram[i][i] + 12.0 * pen_value
    inv = inverse_three(gram)
    for m in range(3):
        for n in range(3):
            numbers[3 * m + n] = inv[m][n]
            numbers[9 + 3 * m + n] = pen_value * inv[m][n]
    numbers[18] = spread(tvw[...].reshape(1, 1)) / pen_value


def project_kernel(dims, e, att, volumes, other, own, to_x, to_y, to_xy, part):
    bins, rows, total, lanes, depth = dims
    c, me, z_base = place(dims)
    b = lax.axis_index("bin")
    a = [[att[bins * m + k] for k in range(bins)] for m in range(3)]
    w = []
    for k in range(4):
        group = b if k < 2 else b ^ 1
        row = []
        for m in range(3):
            value = a[m][k % 2]
            for g in range(1, bins // 2):
                value = jnp.where(group == g, a[m][2 * g + k % 2], value)
            row.append(value)
        w.append(row)

    def body(t, carry):
        tile = pl.ds(pl.multiple_of(t * 8, 8), 8)
        for col in range(lanes // 128):
            at = (tile, slice(128 * col, 128 * col + 128))
            v = [volumes[(0, 2 * c + e, *at)], volumes[(1, 2 * c + e, *at)], other[(0, *at)], other[(1, *at)]]
            for m in range(3):
                part[(m, *at)] = v[0] * w[0][m] + v[1] * w[1][m] + (v[2] * w[2][m] + v[3] * w[3][m])
        return carry

    lax.fori_loop(0, total // 8, body, 0)
    width = rows + 2 * EDGE
    for rel, ref in enumerate((own, to_y, to_x, to_xy)):
        for quarter in range(4):

            @pl.when((me ^ rel) == quarter)
            def _(ref=ref, quarter=quarter):
                start = window_start(quarter, rows, total)
                ref[...] = part[:, start : start + width, :]


def sum_kernel(dims, numbers, *refs):
    parts, (f0, far, near, cross) = (refs[:4], refs[4:8]), refs[8:]
    y = lax.axis_index("slab") % 2
    c = lax.axis_index("bin") % 2
    bins, rows, total, lanes, depth = dims
    inv = [[numbers[3 * m + n] for n in range(3)] for m in range(3)]
    for e in range(2):
        own, from_x, from_y, from_xy = parts[e]
        for to, one, two in ((3 + 4 * y, own, from_x), (7 - 4 * y, from_y, from_xy)):
            for t in range((rows + 2 * EDGE) // 8):
                for col in range(lanes // 128):
                    at = (slice(8 * t, 8 * t + 8), slice(128 * col, 128 * col + 128))
                    d = [one[(m, *at)] + two[(m, *at)] for m in range(3)]
                    for m in range(3):
                        f0[(m, to - 2 * c + e, *at)] = inv[m][0] * d[0] + inv[m][1] * d[1] + inv[m][2] * d[2]
    for core in range(2):

        @pl.when(c == core)
        def _(core=core):
            slab = [f0.at[:, 3 + 4 * k - 2 * core + e] for k in range(2) for e in range(2)]
            far[:, 0] = slab[2 * core][...]
            far[:, 1] = slab[2 * core + 1][...]
            near[:, 0] = slab[2 * (1 - core) + 1 - core][...]
            for at, k in enumerate(((1, 2, 3), (0, 1, 2))[core]):
                cross[:, at] = slab[k][...]


def place(dims):
    bins, rows, total, lanes, depth = dims
    b = lax.axis_index("bin")
    s = lax.axis_index("slab")
    c = b % 2
    return c, 2 * (b // 2) + s % 2, (s // 2) * 8 + 4 * c - 3


def layer_stepper(dims, numbers, fields, dual, down):
    bins, rows, total, lanes, depth = dims
    tiles, columns = (rows + 2 * EDGE) // 8, lanes // 128
    c, me, z_base = place(dims)
    inv = [[numbers[9 + 3 * m + n] for n in range(3)] for m in range(3)]
    twice = [[numbers[9 + 3 * m + n] + numbers[9 + 3 * m + n] for n in range(3)] for m in range(3)]
    threshold = numbers[18]
    squared = threshold * threshold
    lane = lax.broadcasted_iota(jnp.int32, (8, 128), 1)
    sub = lax.broadcasted_iota(jnp.int32, (8, 128), 0)
    last_lane, first_lane = lane == 127, lane == 0
    last_sub, first_sub = sub == 7, sub == 0
    at_end = last_sub & (me == 3)
    zero = jnp.zeros((8, 128), jnp.float32)

    def at(t, col):
        return slice(8 * t, 8 * t + 8), slice(128 * col, 128 * col + 128)

    def layer_step(i, turn):
        src, dst, first = fields[turn], fields[turn + 1], fields[0]
        final = turn == ITERS - 1
        to = i - 2 if final else i
        by = twice if turn == 0 else inv
        z = z_base + i
        above = jnp.where((z >= 0) & (z < depth - 1), i + 1, i)

        def load(ref, m, layer, t, col):
            return ref[(m, layer) + at(t, col)]

        belows = [None] * columns
        for t in range(tiles):
            before = None
            f = [load(src, m, i, t, 0) for m in range(3)]
            f_rolled = [pltpu.roll(f[m], 127, 1) for m in range(3)]
            for col in range(columns):
                following = None
                if t + 1 < tiles:
                    following = [load(src, m, i, t + 1, col) for m in range(3)]
                f_next = f_next_rolled = None
                if col + 1 < columns:
                    f_next = [load(src, m, i, t, col + 1) for m in range(3)]
                    f_next_rolled = [pltpu.roll(f_next[m], 127, 1) for m in range(3)]
                below = belows[col]
                v = []
                for m in range(3):
                    gz = load(src, m, above, t, col) - f[m]
                    up = pltpu.roll(f[m], 7, 0)
                    if following is not None:
                        up = jnp.where(last_sub, pltpu.roll(following[m], 7, 0), up)
                    else:
                        up = jnp.where(at_end, f[m], up)
                    nxt = f[m] if f_next is None else f_next_rolled[m]
                    ahead = jnp.where(last_lane, nxt, f_rolled[m])
                    v.append([gz, up - f[m], ahead - f[m]])
                old = None
                if turn > 0:
                    old = [[load(dual, 3 * m + d, i, t, col) for d in range(3)] for m in range(3)]
                    v = [[v[m][d] + old[m][d] for d in range(3)] for m in range(3)]
                squares = [v[m][0] * v[m][0] + v[m][1] * v[m][1] + v[m][2] * v[m][2] for m in range(3)]
                scale = threshold * lax.rsqrt(jnp.maximum(squares[0] + squares[1] + squares[2], squared))
                if final:
                    scale = scale + scale
                fresh = [[v[m][d] * scale for d in range(3)] for m in range(3)]
                if not final:
                    for m in range(3):
                        for d in range(3):
                            dual[(3 * m + d, i) + at(t, col)] = fresh[m][d]
                if turn == 0:
                    step = fresh
                elif final:
                    step = [[fresh[m][d] - old[m][d] for d in range(3)] for m in range(3)]
                else:
                    step = [[(fresh[m][d] + fresh[m][d]) - old[m][d] for d in range(3)] for m in range(3)]
                lower = [down[(m,) + at(t, col)] for m in range(3)]
                for m in range(3):
                    down[(m,) + at(t, col)] = step[m][0]
                rolled_y = [pltpu.roll(step[m][1], 1, 0) for m in range(3)]
                rolled_x = [pltpu.roll(step[m][2], 1, 1) for m in range(3)]
                rhs = []
                for m in range(3):
                    prev_y = jnp.where(first_sub, zero if below is None else below[m], rolled_y[m])
                    prev_x = jnp.where(first_lane, zero if before is None else before[m], rolled_x[m])
                    div = (step[m][0] - lower[m]) + (step[m][1] - prev_y) + (step[m][2] - prev_x)
                    rhs.append((6.0 if turn == 0 else 12.0) * f[m] + div)
                belows[col], before = rolled_y, rolled_x
                for m in range(3):
                    dst[(m, to) + at(t, col)] = load(first, m, i, t, col) + (
                        by[m][0] * rhs[0] + by[m][1] * rhs[1] + by[m][2] * rhs[2]
                    )
                f, f_rolled = f_next, f_next_rolled

    def run(start, count, turn):
        def body(i, carry):
            layer_step(start + i, turn)
            return carry

        lax.fori_loop(0, count, body, 0)

    def correct(i, turn):
        dst = fields[turn + 1]
        by = twice if turn == 0 else inv
        to = i - 2 if turn == ITERS - 1 else i
        for col in range(columns):
            for t in range(tiles):
                low = [down[(m,) + at(t, col)] for m in range(3)]
                for m in range(3):
                    dst[(m, to) + at(t, col)] = dst[(m, to) + at(t, col)] - (
                        by[m][0] * low[0] + by[m][1] * low[1] + by[m][2] * low[2]
                    )

    return run, correct


def inner_kernel(dims, numbers, cross, held, f0, f1, f2, f3, dual, kept, down):
    c, me, z_base = place(dims)
    for core in range(2):

        @pl.when(c == core)
        def _(core=core):
            for k, to in enumerate(((5, 6, 9), (0, 3, 4))[core]):
                f0[:, to] = cross[:, k]

    run, correct = layer_stepper(dims, numbers, (f0, f1, f2, f3), dual, down)
    for turn in range(ITERS):
        down[...] = jnp.zeros_like(down)
        run(jnp.where(c == 0, 3, 0) + turn, 6 - 2 * turn, turn)
        kept[turn] = down[...]


def outer_kernel(dims, numbers, far, near, g0, g1, g2, g3, gd, kept, f0, f1, f2, f3, dual, o0, o1, o2, o3, down):
    bins, rows, total, lanes, depth = dims
    c, me, z_base = place(dims)
    for core in range(2):

        @pl.when(c == core)
        def _(core=core):
            for k, to in enumerate(((1, 2, 0), (7, 8, 9))[core]):
                f0[:, to] = far[:, k] if k < 2 else near[:, 0]

    run, correct = layer_stepper(dims, numbers, (f0, f1, f2, f3), dual, down)
    for turn in range(ITERS):

        @pl.when(c == 0)
        def _():
            down[...] = jnp.zeros_like(down)

        @pl.when(c == 1)
        def _(turn=turn):
            down[...] = kept[turn]

        run(jnp.where(c == 0, turn, 6 - turn), 3, turn)

        @pl.when(c == 0)
        def _(turn=turn):
            correct(3 + turn, turn)

    twist = twist_of(c, lax.axis_index("slab") // 2, lax.axis_size("slab"))
    for quarter in range(4):

        @pl.when(me == quarter)
        def _(quarter=quarter):
            start = rows * quarter - window_start(quarter, rows, total)
            for key, out in zip(ROUNDS, (o0, o1, o2, o3)):
                out[...] = f3[:, 1 + (key ^ quarter ^ twist), start : start + rows, :]


def twist_of(core, plane, slabs):
    return (TWISTS >> (2 * (4 * core + plane // (slabs // 8)))) & 3


def gather_kernel(rows, r0, r1, r2, r3, out, sem):
    slabs = lax.axis_size("slab")
    z = lax.axis_index("bin") * slabs + lax.axis_index("slab")
    twist = twist_of(z // 4 % 2, z // 8, slabs)
    copies = []
    for n, (t, ref) in enumerate(zip(ROUNDS, (r0, r1, r2, r3))):
        at = pl.multiple_of((z % 4 ^ t ^ twist) * rows, 8)
        copies.append(pltpu.make_async_copy(ref, out.at[:, 0, pl.ds(at, rows), :], sem.at[n]))
        copies[-1].start()
    for copy in copies:
        copy.wait()


def call(kernel, outs, args, spaces=None, scratch=(), aliases=None, flops=0, out_space=VMEM, limit=None):
    shapes = [jax.ShapeDtypeStruct(o, jnp.float32) for o in outs]
    spaces = spaces or [VMEM] * len(args)
    held = sum(math.prod(a.shape) for a in (*shapes, *args, *scratch))
    return pl.pallas_call(
        kernel,
        out_shape=shapes,
        in_specs=[pl.BlockSpec(memory_space=m) for m in spaces],
        out_specs=[pl.BlockSpec(memory_space=m) for m in [out_space] * len(outs)],
        scratch_shapes=list(scratch),
        input_output_aliases=aliases or {},
        cost_estimate=pl.CostEstimate(flops=flops, bytes_accessed=4 * held, transcendentals=0),
        compiler_params=pltpu.CompilerParams(vmem_limit_bytes=limit or 4 * held + (2 << 20)),
    )(*args)


def on_device(mesh_bin, mesh_slab, volumes, attenuation, penalty, tv_weight):
    own_bins, layers, total, lanes = volumes.shape
    bins = own_bins * mesh_bin
    assert mesh_bin == 4 and own_bins == 2 and layers == 4 and mesh_slab % 4 == 0
    rows = total // 4
    width = rows + 2 * EDGE
    depth = layers * mesh_slab
    devices = [(b, s) for b in range(mesh_bin) for s in range(mesh_slab)]

    def send(x, where):
        pairs = []
        for b, s in devices:
            to = where(b, s)
            if 0 <= to[0] < mesh_bin and 0 <= to[1] < mesh_slab:
                pairs.append((b * mesh_slab + s, to[0] * mesh_slab + to[1]))
        return lax.ppermute(x, ("bin", "slab"), pairs)

    dims = (bins, rows, total, lanes, depth)
    spreads = jnp.broadcast_to(attenuation.T.reshape(3 * bins, 1, 1), (3 * bins, 8, 128))
    away = call(
        away_kernel,
        [(2, total, lanes)] * 2,
        (volumes,),
        [pl.ANY],
        [pltpu.SemaphoreType.DMA((2, 2))],
        limit=GRANT - 6 * 2 * total * lanes * 4,
    )
    others = [send(part, lambda b, s: (b ^ 1, s)) for part in away]
    win = (3, 2, width, lanes)
    parts = []
    for e, other in enumerate(others):
        own, to_x, to_y, to_xy = call(
            functools.partial(project_kernel, dims, e),
            [(3, width, lanes)] * 4,
            (spreads, volumes, other),
            scratch=[VMEM((3, total, lanes), jnp.float32)],
        )
        from_xy = send(to_xy, lambda b, s: (b ^ 2, s ^ 1))
        from_x = send(to_x, lambda b, s: (b ^ 2, s))
        from_y = send(to_y, lambda b, s: (b, s ^ 1))
        parts += [own, from_x, from_y, from_xy]
    numbers = call(
        functools.partial(ready_kernel, bins), [(19, 8, 128)], (penalty, tv_weight, spreads)
    )[0]
    state = [(3, 10, width, lanes)] * 3 + [(3, 5, width, lanes), (9, 9, width, lanes)]
    f0, far, near, cross = call(
        functools.partial(sum_kernel, dims),
        [state[0], win, (3, 1, width, lanes), (3, 3, width, lanes)],
        (numbers, *parts),
    )
    far = send(far, lambda b, s: (b ^ 1, s + (2 if b % 2 else -2)))
    near = send(near, lambda b, s: (b, s + (-2 if b % 2 else 2)))
    cross = send(cross, lambda b, s: (b ^ 1, s))
    work = 150 * width * lanes
    scratch = [VMEM((3, width, lanes), jnp.float32)]
    inner = call(
        functools.partial(inner_kernel, dims),
        state + [(3, 3, width, lanes)],
        (numbers, cross, f0),
        None,
        scratch,
        {2: 0},
        12 * work,
    )
    blocks = call(
        functools.partial(outer_kernel, dims),
        state + [(3, rows, lanes)] * 4,
        (numbers, far, near, *inner),
        None,
        scratch,
        {3 + i: i for i in range(5)},
        9 * work,
    )[5:]

    def owner(t):
        def where(b, s):
            j = t ^ (2 * (b // 2) + s % 2) ^ twist_of(b % 2, s // 2, mesh_slab)
            z = (s // 2) * 8 + 4 * (b % 2) + j
            return z // mesh_slab, z % mesh_slab

        return where

    blocks = [send(block, owner(key)) for key, block in zip(ROUNDS, blocks)]
    return call(
        functools.partial(gather_kernel, rows),
        [(3, 1, total, lanes)],
        blocks,
        scratch=[pltpu.SemaphoreType.DMA((4,))],
        out_space=pl.ANY,
    )[0]


def solution(mesh):
    placed = (P("bin", "slab", None, None), P(), P(), P())
    return jax.shard_map(
        functools.partial(on_device, mesh.shape["bin"], mesh.shape["slab"]),
        mesh=mesh,
        in_specs=placed,
        out_specs=P(None, ("bin", "slab"), None, None),
        check_vma=False,
    )
```

```python
import functools
import math

import jax
import jax.numpy as jnp
from jax import lax
from jax.experimental import pallas as pl
from jax.experimental.pallas import tpu as pltpu
from jax.sharding import PartitionSpec as P


ITERS = 3
EDGE = 4
GRANT = 56_000 * 1024
ROUNDS = (1, 3, 0, 2)
TWISTS = 32770
VMEM = pltpu.VMEM


def window_start(quarter, rows, total):
    return min(max(rows * quarter - EDGE, 0), total - rows - 2 * EDGE)


def inverse_three(m):
    cof = [
        [
            m[(r + 1) % 3][(c + 1) % 3] * m[(r + 2) % 3][(c + 2) % 3]
            - m[(r + 1) % 3][(c + 2) % 3] * m[(r + 2) % 3][(c + 1) % 3]
            for c in range(3)
        ]
        for r in range(3)
    ]
    det = m[0][0] * cof[0][0] + m[0][1] * cof[0][1] + m[0][2] * cof[0][2]
    over = 1.0 / det
    return [[cof[c][r] * over for c in range(3)] for r in range(3)]


def away_kernel(volumes, first, second, sem):
    c = lax.axis_index("bin") % 2
    copies = [
        pltpu.make_async_copy(volumes.at[k, 2 * (1 - c) + e], ref.at[k], sem.at[e, k])
        for e, ref in enumerate((first, second))
        for k in range(2)
    ]
    for copy in copies:
        copy.start()
    for copy in copies:
        copy.wait()


def spread(x):
    return jnp.broadcast_to(x, (8, 128))


def ready_kernel(bins, pen, tvw, att, numbers):
    a = [[att[bins * m + k] for k in range(bins)] for m in range(3)]
    pen_value = spread(pen[...].reshape(1, 1))
    gram = [[None] * 3 for _ in range(3)]
    for i in range(3):
        for j in range(i, 3):
            total = a[i][0] * a[j][0]
            for k in range(1, bins):
                total = total + a[i][k] * a[j][k]
            gram[i][j] = gram[j][i] = total
    for i in range(3):
        gram[i][i] = gram[i][i] + 12.0 * pen_value
    inv = inverse_three(gram)
    for m in range(3):
        for n in range(3):
            numbers[3 * m + n] = inv[m][n]
            numbers[9 + 3 * m + n] = pen_value * inv[m][n]
    numbers[18] = spread(tvw[...].reshape(1, 1)) / pen_value


def project_kernel(dims, e, att, volumes, other, own, to_x, to_y, to_xy, part):
    bins, rows, total, lanes, _ = dims
    c, me, _ = place()
    b = lax.axis_index("bin")
    a = [[att[bins * m + k] for k in range(bins)] for m in range(3)]
    w = []
    for k in range(4):
        group = b if k < 2 else b ^ 1
        row = []
        for m in range(3):
            value = a[m][k % 2]
            for g in range(1, bins // 2):
                value = jnp.where(group == g, a[m][2 * g + k % 2], value)
            row.append(value)
        w.append(row)

    def body(t, carry):
        tile = pl.ds(pl.multiple_of(t * 8, 8), 8)
        for col in range(lanes // 128):
            at = (tile, slice(128 * col, 128 * col + 128))
            v = [volumes[(0, 2 * c + e, *at)], volumes[(1, 2 * c + e, *at)], other[(0, *at)], other[(1, *at)]]
            for m in range(3):
                part[(m, *at)] = v[0] * w[0][m] + v[1] * w[1][m] + (v[2] * w[2][m] + v[3] * w[3][m])
        return carry

    lax.fori_loop(0, total // 8, body, 0)
    width = rows + 2 * EDGE
    for rel, ref in enumerate((own, to_y, to_x, to_xy)):
        for quarter in range(4):

            @pl.when((me ^ rel) == quarter)
            def _(ref=ref, quarter=quarter):
                start = window_start(quarter, rows, total)
                ref[...] = part[:, start : start + width, :]


def sum_kernel(dims, numbers, *refs):
    parts, (f0, far, near, cross) = (refs[:4], refs[4:8]), refs[8:]
    y = lax.axis_index("slab") % 2
    c = lax.axis_index("bin") % 2
    _, rows, _, lanes, _ = dims
    inv = [[numbers[3 * m + n] for n in range(3)] for m in range(3)]
    for e in range(2):
        own, from_x, from_y, from_xy = parts[e]
        for to, one, two in ((3 + 4 * y, own, from_x), (7 - 4 * y, from_y, from_xy)):
            for t in range((rows + 2 * EDGE) // 8):
                for col in range(lanes // 128):
                    at = (slice(8 * t, 8 * t + 8), slice(128 * col, 128 * col + 128))
                    d = [one[(m, *at)] + two[(m, *at)] for m in range(3)]
                    for m in range(3):
                        f0[(m, to - 2 * c + e, *at)] = inv[m][0] * d[0] + inv[m][1] * d[1] + inv[m][2] * d[2]
    for core in range(2):

        @pl.when(c == core)
        def _(core=core):
            slab = [f0.at[:, 3 + 4 * k - 2 * core + e] for k in range(2) for e in range(2)]
            far[:, 0] = slab[2 * core][...]
            far[:, 1] = slab[2 * core + 1][...]
            near[:, 0] = slab[2 * (1 - core) + 1 - core][...]
            for at, k in enumerate(((1, 2, 3), (0, 1, 2))[core]):
                cross[:, at] = slab[k][...]


def place():
    b = lax.axis_index("bin")
    s = lax.axis_index("slab")
    c = b % 2
    return c, 2 * (b // 2) + s % 2, (s // 2) * 8 + 4 * c - 3


def layer_stepper(dims, numbers, fields, dual, down):
    _, rows, _, lanes, depth = dims
    tiles, columns = (rows + 2 * EDGE) // 8, lanes // 128
    _, me, z_base = place()
    inv = [[numbers[9 + 3 * m + n] for n in range(3)] for m in range(3)]
    twice = [[numbers[9 + 3 * m + n] + numbers[9 + 3 * m + n] for n in range(3)] for m in range(3)]
    threshold = numbers[18]
    squared = threshold * threshold
    lane = lax.broadcasted_iota(jnp.int32, (8, 128), 1)
    sub = lax.broadcasted_iota(jnp.int32, (8, 128), 0)
    last_lane, first_lane = lane == 127, lane == 0
    last_sub, first_sub = sub == 7, sub == 0
    at_end = last_sub & (me == 3)
    zero = jnp.zeros((8, 128), jnp.float32)

    def at(t, col):
        return slice(8 * t, 8 * t + 8), slice(128 * col, 128 * col + 128)

    def layer_step(i, turn):
        src, dst, first = fields[turn], fields[turn + 1], fields[0]
        final = turn == ITERS - 1
        to = i - 2 if final else i
        by = twice if turn == 0 else inv
        z = z_base + i
        above = jnp.where((z >= 0) & (z < depth - 1), i + 1, i)

        def load(ref, m, layer, t, col):
            return ref[(m, layer) + at(t, col)]

        belows = [None] * columns
        for t in range(tiles):
            before = None
            f = [load(src, m, i, t, 0) for m in range(3)]
            f_rolled = [pltpu.roll(f[m], 127, 1) for m in range(3)]
            for col in range(columns):
                following = None
                if t + 1 < tiles:
                    following = [load(src, m, i, t + 1, col) for m in range(3)]
                f_next = f_next_rolled = None
                if col + 1 < columns:
                    f_next = [load(src, m, i, t, col + 1) for m in range(3)]
                    f_next_rolled = [pltpu.roll(f_next[m], 127, 1) for m in range(3)]
                below = belows[col]
                v = []
                for m in range(3):
                    gz = load(src, m, above, t, col) - f[m]
                    up = pltpu.roll(f[m], 7, 0)
                    if following is not None:
                        up = jnp.where(last_sub, pltpu.roll(following[m], 7, 0), up)
                    else:
                        up = jnp.where(at_end, f[m], up)
                    nxt = f[m] if f_next is None else f_next_rolled[m]
                    ahead = jnp.where(last_lane, nxt, f_rolled[m])
                    v.append([gz, up - f[m], ahead - f[m]])
                old = None
                if turn > 0:
                    old = [[load(dual, 3 * m + d, i, t, col) for d in range(3)] for m in range(3)]
                    v = [[v[m][d] + old[m][d] for d in range(3)] for m in range(3)]
                squares = [v[m][0] * v[m][0] + v[m][1] * v[m][1] + v[m][2] * v[m][2] for m in range(3)]
                scale = threshold * lax.rsqrt(jnp.maximum(squares[0] + squares[1] + squares[2], squared))
                if final:
                    scale = scale + scale
                fresh = [[v[m][d] * scale for d in range(3)] for m in range(3)]
                if not final:
                    for m in range(3):
                        for d in range(3):
                            dual[(3 * m + d, i) + at(t, col)] = fresh[m][d]
                if turn == 0:
                    step = fresh
                elif final:
                    step = [[fresh[m][d] - old[m][d] for d in range(3)] for m in range(3)]
                else:
                    step = [[(fresh[m][d] + fresh[m][d]) - old[m][d] for d in range(3)] for m in range(3)]
                lower = [down[(m,) + at(t, col)] for m in range(3)]
                for m in range(3):
                    down[(m,) + at(t, col)] = step[m][0]
                rolled_y = [pltpu.roll(step[m][1], 1, 0) for m in range(3)]
                rolled_x = [pltpu.roll(step[m][2], 1, 1) for m in range(3)]
                rhs = []
                for m in range(3):
                    prev_y = jnp.where(first_sub, zero if below is None else below[m], rolled_y[m])
                    prev_x = jnp.where(first_lane, zero if before is None else before[m], rolled_x[m])
                    div = (step[m][0] - lower[m]) + (step[m][1] - prev_y) + (step[m][2] - prev_x)
                    rhs.append((6.0 if turn == 0 else 12.0) * f[m] + div)
                belows[col], before = rolled_y, rolled_x
                for m in range(3):
                    dst[(m, to) + at(t, col)] = load(first, m, i, t, col) + (
                        by[m][0] * rhs[0] + by[m][1] * rhs[1] + by[m][2] * rhs[2]
                    )
                f, f_rolled = f_next, f_next_rolled

    def run(start, count, turn):
        def body(i, carry):
            layer_step(start + i, turn)
            return carry

        lax.fori_loop(0, count, body, 0)

    def correct(i, turn):
        dst = fields[turn + 1]
        by = twice if turn == 0 else inv
        to = i - 2 if turn == ITERS - 1 else i
        for col in range(columns):
            for t in range(tiles):
                low = [down[(m,) + at(t, col)] for m in range(3)]
                for m in range(3):
                    dst[(m, to) + at(t, col)] = dst[(m, to) + at(t, col)] - (
                        by[m][0] * low[0] + by[m][1] * low[1] + by[m][2] * low[2]
                    )

    return run, correct


def inner_kernel(dims, numbers, cross, held, f0, f1, f2, f3, dual, kept, down):
    c, _, _ = place()
    for core in range(2):

        @pl.when(c == core)
        def _(core=core):
            for k, to in enumerate(((5, 6, 9), (0, 3, 4))[core]):
                f0[:, to] = cross[:, k]

    run, _ = layer_stepper(dims, numbers, (f0, f1, f2, f3), dual, down)
    for turn in range(ITERS):
        down[...] = jnp.zeros_like(down)
        run(jnp.where(c == 0, 3, 0) + turn, 6 - 2 * turn, turn)
        kept[turn] = down[...]


def outer_kernel(dims, numbers, far, near, g0, g1, g2, g3, gd, kept, f0, f1, f2, f3, dual, o0, o1, o2, o3, down):
    _, rows, total, _, _ = dims
    c, me, _ = place()
    for core in range(2):

        @pl.when(c == core)
        def _(core=core):
            for k, to in enumerate(((1, 2, 0), (7, 8, 9))[core]):
                f0[:, to] = far[:, k] if k < 2 else near[:, 0]

    run, correct = layer_stepper(dims, numbers, (f0, f1, f2, f3), dual, down)
    for turn in range(ITERS):

        @pl.when(c == 0)
        def _():
            down[...] = jnp.zeros_like(down)

        @pl.when(c == 1)
        def _(turn=turn):
            down[...] = kept[turn]

        run(jnp.where(c == 0, turn, 6 - turn), 3, turn)

        @pl.when(c == 0)
        def _(turn=turn):
            correct(3 + turn, turn)

    twist = twist_of(c, lax.axis_index("slab") // 2, lax.axis_size("slab"))
    for quarter in range(4):

        @pl.when(me == quarter)
        def _(quarter=quarter):
            start = rows * quarter - window_start(quarter, rows, total)
            for key, out in zip(ROUNDS, (o0, o1, o2, o3)):
                out[...] = f3[:, 1 + (key ^ quarter ^ twist), start : start + rows, :]


def twist_of(core, plane, slabs):
    return (TWISTS >> (2 * (4 * core + plane // (slabs // 8)))) & 3


def gather_kernel(rows, r0, r1, r2, r3, out, sem):
    slabs = lax.axis_size("slab")
    z = lax.axis_index("bin") * slabs + lax.axis_index("slab")
    twist = twist_of(z // 4 % 2, z // 8, slabs)
    copies = []
    for n, (t, ref) in enumerate(zip(ROUNDS, (r0, r1, r2, r3))):
        at = pl.multiple_of((z % 4 ^ t ^ twist) * rows, 8)
        copies.append(pltpu.make_async_copy(ref, out.at[:, 0, pl.ds(at, rows), :], sem.at[n]))
        copies[-1].start()
    for copy in copies:
        copy.wait()


def call(kernel, outs, args, spaces=None, scratch=(), aliases=None, flops=0, out_space=VMEM, limit=None):
    shapes = [jax.ShapeDtypeStruct(o, jnp.float32) for o in outs]
    spaces = spaces or [VMEM] * len(args)
    held = sum(math.prod(a.shape) for a in (*shapes, *args, *scratch))
    return pl.pallas_call(
        kernel,
        out_shape=shapes,
        in_specs=[pl.BlockSpec(memory_space=m) for m in spaces],
        out_specs=[pl.BlockSpec(memory_space=m) for m in [out_space] * len(outs)],
        scratch_shapes=list(scratch),
        input_output_aliases=aliases or {},
        cost_estimate=pl.CostEstimate(flops=flops, bytes_accessed=4 * held, transcendentals=0),
        compiler_params=pltpu.CompilerParams(vmem_limit_bytes=limit or 4 * held + (2 << 20)),
    )(*args)


def on_device(mesh_bin, mesh_slab, volumes, attenuation, penalty, tv_weight):
    own_bins, layers, total, lanes = volumes.shape
    bins = own_bins * mesh_bin
    assert mesh_bin == 4 and own_bins == 2 and layers == 4 and mesh_slab % 4 == 0
    rows = total // 4
    width = rows + 2 * EDGE
    depth = layers * mesh_slab
    devices = [(b, s) for b in range(mesh_bin) for s in range(mesh_slab)]

    def send(x, where):
        pairs = []
        for b, s in devices:
            to = where(b, s)
            if 0 <= to[0] < mesh_bin and 0 <= to[1] < mesh_slab:
                pairs.append((b * mesh_slab + s, to[0] * mesh_slab + to[1]))
        return lax.ppermute(x, ("bin", "slab"), pairs)

    dims = (bins, rows, total, lanes, depth)
    spreads = jnp.broadcast_to(attenuation.T.reshape(3 * bins, 1, 1), (3 * bins, 8, 128))
    away = call(
        away_kernel,
        [(2, total, lanes)] * 2,
        (volumes,),
        [pl.ANY],
        [pltpu.SemaphoreType.DMA((2, 2))],
        limit=GRANT - 6 * 2 * total * lanes * 4,
    )
    others = [send(part, lambda b, s: (b ^ 1, s)) for part in away]
    win = (3, 2, width, lanes)
    parts = []
    for e, other in enumerate(others):
        own, to_x, to_y, to_xy = call(
            functools.partial(project_kernel, dims, e),
            [(3, width, lanes)] * 4,
            (spreads, volumes, other),
            scratch=[VMEM((3, total, lanes), jnp.float32)],
        )
        from_xy = send(to_xy, lambda b, s: (b ^ 2, s ^ 1))
        from_x = send(to_x, lambda b, s: (b ^ 2, s))
        from_y = send(to_y, lambda b, s: (b, s ^ 1))
        parts += [own, from_x, from_y, from_xy]
    numbers = call(
        functools.partial(ready_kernel, bins), [(19, 8, 128)], (penalty, tv_weight, spreads)
    )[0]
    state = [(3, 10, width, lanes)] * 3 + [(3, 5, width, lanes), (9, 9, width, lanes)]
    f0, far, near, cross = call(
        functools.partial(sum_kernel, dims),
        [state[0], win, (3, 1, width, lanes), (3, 3, width, lanes)],
        (numbers, *parts),
    )
    far = send(far, lambda b, s: (b ^ 1, s + (2 if b % 2 else -2)))
    near = send(near, lambda b, s: (b, s + (-2 if b % 2 else 2)))
    cross = send(cross, lambda b, s: (b ^ 1, s))
    work = 150 * width * lanes
    scratch = [VMEM((3, width, lanes), jnp.float32)]
    inner = call(
        functools.partial(inner_kernel, dims),
        state + [(3, 3, width, lanes)],
        (numbers, cross, f0),
        None,
        scratch,
        {2: 0},
        12 * work,
    )
    blocks = call(
        functools.partial(outer_kernel, dims),
        state + [(3, rows, lanes)] * 4,
        (numbers, far, near, *inner),
        None,
        scratch,
        {3 + i: i for i in range(5)},
        9 * work,
    )[5:]

    def owner(t):
        def where(b, s):
            j = t ^ (2 * (b // 2) + s % 2) ^ twist_of(b % 2, s // 2, mesh_slab)
            z = (s // 2) * 8 + 4 * (b % 2) + j
            return z // mesh_slab, z % mesh_slab

        return where

    blocks = [send(block, owner(key)) for key, block in zip(ROUNDS, blocks)]
    return call(
        functools.partial(gather_kernel, rows),
        [(3, 1, total, lanes)],
        blocks,
        scratch=[pltpu.SemaphoreType.DMA((4,))],
        out_space=pl.ANY,
    )[0]


def solution(mesh):
    placed = (P("bin", "slab", None, None), P(), P(), P())
    return jax.shard_map(
        functools.partial(on_device, mesh.shape["bin"], mesh.shape["slab"]),
        mesh=mesh,
        in_specs=placed,
        out_specs=P(None, ("bin", "slab"), None, None),
        check_vma=False,
    )
```

```python
import functools
import math

import jax
import jax.numpy as jnp
from jax import lax
from jax.experimental import pallas as pl
from jax.experimental.pallas import tpu as pltpu
from jax.sharding import PartitionSpec as P


ITERS = 3
EDGE = 4
GRANT = 56_000 * 1024
ROUNDS = (1, 3, 0, 2)
TWISTS = 32770
VMEM = pltpu.VMEM


def window_start(quarter, rows, total):
    return min(max(rows * quarter - EDGE, 0), total - rows - 2 * EDGE)


def inverse_three(m):
    cof = [
        [
            m[(r + 1) % 3][(c + 1) % 3] * m[(r + 2) % 3][(c + 2) % 3]
            - m[(r + 1) % 3][(c + 2) % 3] * m[(r + 2) % 3][(c + 1) % 3]
            for c in range(3)
        ]
        for r in range(3)
    ]
    det = m[0][0] * cof[0][0] + m[0][1] * cof[0][1] + m[0][2] * cof[0][2]
    over = 1.0 / det
    return [[cof[c][r] * over for c in range(3)] for r in range(3)]


def away_kernel(volumes, first, second, sem):
    c = lax.axis_index("bin") % 2
    copies = [
        pltpu.make_async_copy(volumes.at[k, 2 * (1 - c) + e], ref.at[k], sem.at[e, k])
        for e, ref in enumerate((first, second))
        for k in range(2)
    ]
    for copy in copies:
        copy.start()
    for copy in copies:
        copy.wait()


def spread(x):
    return jnp.broadcast_to(x, (8, 128))


def ready_kernel(bins, pen, tvw, att, numbers):
    a = [[att[bins * m + k] for k in range(bins)] for m in range(3)]
    pen_value = spread(pen[...].reshape(1, 1))
    gram = [[None] * 3 for _ in range(3)]
    for i in range(3):
        for j in range(i, 3):
            total = a[i][0] * a[j][0]
            for k in range(1, bins):
                total = total + a[i][k] * a[j][k]
            gram[i][j] = gram[j][i] = total
    for i in range(3):
        gram[i][i] = gram[i][i] + 12.0 * pen_value
    inv = inverse_three(gram)
    for m in range(3):
        for n in range(3):
            numbers[3 * m + n] = inv[m][n]
            numbers[9 + 3 * m + n] = pen_value * inv[m][n]
    numbers[18] = spread(tvw[...].reshape(1, 1)) / pen_value


def project_kernel(dims, e, att, volumes, other, own, to_x, to_y, to_xy, part):
    bins, rows, total, lanes, _ = dims
    c, me, _ = place()
    b = lax.axis_index("bin")
    a = [[att[bins * m + k] for k in range(bins)] for m in range(3)]
    w = []
    for k in range(4):
        group = b if k < 2 else b ^ 1
        row = []
        for m in range(3):
            value = a[m][k % 2]
            for g in range(1, bins // 2):
                value = jnp.where(group == g, a[m][2 * g + k % 2], value)
            row.append(value)
        w.append(row)

    def body(t, carry):
        tile = pl.ds(pl.multiple_of(t * 8, 8), 8)
        for col in range(lanes // 128):
            at = (tile, slice(128 * col, 128 * col + 128))
            v = [volumes[(0, 2 * c + e, *at)], volumes[(1, 2 * c + e, *at)], other[(0, *at)], other[(1, *at)]]
            for m in range(3):
                part[(m, *at)] = v[0] * w[0][m] + v[1] * w[1][m] + (v[2] * w[2][m] + v[3] * w[3][m])
        return carry

    lax.fori_loop(0, total // 8, body, 0)
    width = rows + 2 * EDGE
    for rel, ref in enumerate((own, to_y, to_x, to_xy)):
        for quarter in range(4):

            @pl.when((me ^ rel) == quarter)
            def _(ref=ref, quarter=quarter):
                start = window_start(quarter, rows, total)
                ref[...] = part[:, start : start + width, :]


def sum_kernel(dims, numbers, *refs):
    parts, (f0, far, near, cross) = (refs[:4], refs[4:8]), refs[8:]
    y = lax.axis_index("slab") % 2
    c = lax.axis_index("bin") % 2
    _, rows, _, lanes, _ = dims
    inv = [[numbers[3 * m + n] for n in range(3)] for m in range(3)]
    for e in range(2):
        own, from_x, from_y, from_xy = parts[e]
        for to, one, two in ((3 + 4 * y, own, from_x), (7 - 4 * y, from_y, from_xy)):
            for t in range((rows + 2 * EDGE) // 8):
                for col in range(lanes // 128):
                    at = (slice(8 * t, 8 * t + 8), slice(128 * col, 128 * col + 128))
                    d = [one[(m, *at)] + two[(m, *at)] for m in range(3)]
                    for m in range(3):
                        f0[(m, to - 2 * c + e, *at)] = inv[m][0] * d[0] + inv[m][1] * d[1] + inv[m][2] * d[2]
    for core in range(2):

        @pl.when(c == core)
        def _(core=core):
            slab = [f0.at[:, 3 + 4 * k - 2 * core + e] for k in range(2) for e in range(2)]
            far[:, 0] = slab[2 * core][...]
            far[:, 1] = slab[2 * core + 1][...]
            near[:, 0] = slab[2 * (1 - core) + 1 - core][...]
            for at, k in enumerate(((1, 2, 3), (0, 1, 2))[core]):
                cross[:, at] = slab[k][...]


def place():
    b = lax.axis_index("bin")
    s = lax.axis_index("slab")
    c = b % 2
    return c, 2 * (b // 2) + s % 2, (s // 2) * 8 + 4 * c - 3


def layer_stepper(dims, numbers, fields, dual, down):
    _, rows, _, lanes, depth = dims
    tiles, columns = (rows + 2 * EDGE) // 8, lanes // 128
    _, me, z_base = place()
    inv = [[numbers[9 + 3 * m + n] for n in range(3)] for m in range(3)]
    twice = [[numbers[9 + 3 * m + n] + numbers[9 + 3 * m + n] for n in range(3)] for m in range(3)]
    threshold = numbers[18]
    squared = threshold * threshold
    lane = lax.broadcasted_iota(jnp.int32, (8, 128), 1)
    sub = lax.broadcasted_iota(jnp.int32, (8, 128), 0)
    last_lane, first_lane = lane == 127, lane == 0
    last_sub, first_sub = sub == 7, sub == 0
    at_end = last_sub & (me == 3)
    zero = jnp.zeros((8, 128), jnp.float32)

    def at(t, col):
        return slice(8 * t, 8 * t + 8), slice(128 * col, 128 * col + 128)

    def layer_step(i, turn):
        src, dst, first = fields[turn], fields[turn + 1], fields[0]
        final = turn == ITERS - 1
        to = i - 2 if final else i
        by = twice if turn == 0 else inv
        z = z_base + i
        above = jnp.where((z >= 0) & (z < depth - 1), i + 1, i)

        def load(ref, m, layer, t, col):
            return ref[(m, layer) + at(t, col)]

        belows = [None] * columns
        for t in range(tiles):
            before = None
            f = [load(src, m, i, t, 0) for m in range(3)]
            f_rolled = [pltpu.roll(f[m], 127, 1) for m in range(3)]
            for col in range(columns):
                following = None
                if t + 1 < tiles:
                    following = [load(src, m, i, t + 1, col) for m in range(3)]
                f_next = f_next_rolled = None
                if col + 1 < columns:
                    f_next = [load(src, m, i, t, col + 1) for m in range(3)]
                    f_next_rolled = [pltpu.roll(f_next[m], 127, 1) for m in range(3)]
                below = belows[col]
                v = []
                for m in range(3):
                    gz = load(src, m, above, t, col) - f[m]
                    up = pltpu.roll(f[m], 7, 0)
                    if following is not None:
                        up = jnp.where(last_sub, pltpu.roll(following[m], 7, 0), up)
                    else:
                        up = jnp.where(at_end, f[m], up)
                    nxt = f[m] if f_next is None else f_next_rolled[m]
                    ahead = jnp.where(last_lane, nxt, f_rolled[m])
                    v.append([gz, up - f[m], ahead - f[m]])
                old = None
                if turn > 0:
                    old = [[load(dual, 3 * m + d, i, t, col) for d in range(3)] for m in range(3)]
                    v = [[v[m][d] + old[m][d] for d in range(3)] for m in range(3)]
                squares = [v[m][0] * v[m][0] + v[m][1] * v[m][1] + v[m][2] * v[m][2] for m in range(3)]
                scale = threshold * lax.rsqrt(jnp.maximum(squares[0] + squares[1] + squares[2], squared))
                if final:
                    scale = scale + scale
                fresh = [[v[m][d] * scale for d in range(3)] for m in range(3)]
                if not final:
                    for m in range(3):
                        for d in range(3):
                            dual[(3 * m + d, i) + at(t, col)] = fresh[m][d]
                if turn == 0:
                    step = fresh
                elif final:
                    step = [[fresh[m][d] - old[m][d] for d in range(3)] for m in range(3)]
                else:
                    step = [[(fresh[m][d] + fresh[m][d]) - old[m][d] for d in range(3)] for m in range(3)]
                lower = [down[(m,) + at(t, col)] for m in range(3)]
                for m in range(3):
                    down[(m,) + at(t, col)] = step[m][0]
                rolled_y = [pltpu.roll(step[m][1], 1, 0) for m in range(3)]
                rolled_x = [pltpu.roll(step[m][2], 1, 1) for m in range(3)]
                rhs = []
                for m in range(3):
                    prev_y = jnp.where(first_sub, zero if below is None else below[m], rolled_y[m])
                    prev_x = jnp.where(first_lane, zero if before is None else before[m], rolled_x[m])
                    div = (step[m][0] - lower[m]) + (step[m][1] - prev_y) + (step[m][2] - prev_x)
                    rhs.append((6.0 if turn == 0 else 12.0) * f[m] + div)
                belows[col], before = rolled_y, rolled_x
                for m in range(3):
                    dst[(m, to) + at(t, col)] = load(first, m, i, t, col) + (
                        by[m][0] * rhs[0] + by[m][1] * rhs[1] + by[m][2] * rhs[2]
                    )
                f, f_rolled = f_next, f_next_rolled

    def run(start, count, turn):
        def body(i, carry):
            layer_step(start + i, turn)
            return carry

        lax.fori_loop(0, count, body, 0)

    def correct(i, turn):
        dst = fields[turn + 1]
        by = twice if turn == 0 else inv
        to = i - 2 if turn == ITERS - 1 else i
        for col in range(columns):
            for t in range(tiles):
                low = [down[(m,) + at(t, col)] for m in range(3)]
                for m in range(3):
                    dst[(m, to) + at(t, col)] = dst[(m, to) + at(t, col)] - (
                        by[m][0] * low[0] + by[m][1] * low[1] + by[m][2] * low[2]
                    )

    return run, correct


def inner_kernel(dims, numbers, cross, held, f0, f1, f2, f3, dual, kept, down):
    c, _, _ = place()
    for core in range(2):

        @pl.when(c == core)
        def _(core=core):
            for k, to in enumerate(((5, 6, 9), (0, 3, 4))[core]):
                f0[:, to] = cross[:, k]

    run, _ = layer_stepper(dims, numbers, (f0, f1, f2, f3), dual, down)
    for turn in range(ITERS):
        down[...] = jnp.zeros_like(down)
        run(jnp.where(c == 0, 3, 0) + turn, 6 - 2 * turn, turn)
        kept[turn] = down[...]


def outer_kernel(dims, numbers, far, near, g0, g1, g2, g3, gd, kept, f0, f1, f2, f3, dual, o0, o1, o2, o3, down):
    _, rows, total, _, _ = dims
    c, me, _ = place()
    for core in range(2):

        @pl.when(c == core)
        def _(core=core):
            for k, to in enumerate(((1, 2, 0), (7, 8, 9))[core]):
                f0[:, to] = far[:, k] if k < 2 else near[:, 0]

    run, correct = layer_stepper(dims, numbers, (f0, f1, f2, f3), dual, down)
    for turn in range(ITERS):

        @pl.when(c == 0)
        def _():
            down[...] = jnp.zeros_like(down)

        @pl.when(c == 1)
        def _(turn=turn):
            down[...] = kept[turn]

        run(jnp.where(c == 0, turn, 6 - turn), 3, turn)

        @pl.when(c == 0)
        def _(turn=turn):
            correct(3 + turn, turn)

    twist = twist_of(c, lax.axis_index("slab") // 2, lax.axis_size("slab"))
    for quarter in range(4):

        @pl.when(me == quarter)
        def _(quarter=quarter):
            start = rows * quarter - window_start(quarter, rows, total)
            for key, out in zip(ROUNDS, (o0, o1, o2, o3)):
                out[...] = f3[:, 1 + (key ^ quarter ^ twist), start : start + rows, :]


def twist_of(core, plane, slabs):
    return (TWISTS >> (2 * (4 * core + plane // (slabs // 8)))) & 3


def gather_kernel(rows, keys, *refs):
    blocks, (out, sem) = refs[: len(keys)], refs[-2:]
    slabs = lax.axis_size("slab")
    z = lax.axis_index("bin") * slabs + lax.axis_index("slab")
    twist = twist_of(z // 4 % 2, z // 8, slabs)
    copies = []
    for n, (t, ref) in enumerate(zip(keys, blocks)):
        at = pl.multiple_of((z % 4 ^ t ^ twist) * rows, 8)
        copies.append(pltpu.make_async_copy(ref, out.at[:, 0, pl.ds(at, rows), :], sem.at[n]))
        copies[-1].start()
    for copy in copies:
        copy.wait()


def call(kernel, outs, args, spaces=None, scratch=(), aliases=None, flops=0, out_space=VMEM, limit=None):
    shapes = [jax.ShapeDtypeStruct(o, jnp.float32) for o in outs]
    spaces = spaces or [VMEM] * len(args)
    held = sum(math.prod(a.shape) for a in (*shapes, *args, *scratch))
    return pl.pallas_call(
        kernel,
        out_shape=shapes,
        in_specs=[pl.BlockSpec(memory_space=m) for m in spaces],
        out_specs=[pl.BlockSpec(memory_space=m) for m in [out_space] * len(outs)],
        scratch_shapes=list(scratch),
        input_output_aliases=aliases or {},
        cost_estimate=pl.CostEstimate(flops=flops, bytes_accessed=4 * held, transcendentals=0),
        compiler_params=pltpu.CompilerParams(vmem_limit_bytes=limit or 4 * held + (2 << 20)),
    )(*args)


def on_device(mesh_bin, mesh_slab, volumes, attenuation, penalty, tv_weight):
    own_bins, layers, total, lanes = volumes.shape
    bins = own_bins * mesh_bin
    assert mesh_bin == 4 and own_bins == 2 and layers == 4 and mesh_slab % 4 == 0
    rows = total // 4
    width = rows + 2 * EDGE
    depth = layers * mesh_slab
    devices = [(b, s) for b in range(mesh_bin) for s in range(mesh_slab)]

    def send(x, where):
        pairs = []
        for b, s in devices:
            to = where(b, s)
            if 0 <= to[0] < mesh_bin and 0 <= to[1] < mesh_slab:
                pairs.append((b * mesh_slab + s, to[0] * mesh_slab + to[1]))
        return lax.ppermute(x, ("bin", "slab"), pairs)

    dims = (bins, rows, total, lanes, depth)
    spreads = jnp.broadcast_to(attenuation.T.reshape(3 * bins, 1, 1), (3 * bins, 8, 128))
    away = call(
        away_kernel,
        [(2, total, lanes)] * 2,
        (volumes,),
        [pl.ANY],
        [pltpu.SemaphoreType.DMA((2, 2))],
        limit=GRANT - 6 * 2 * total * lanes * 4,
    )
    others = [send(part, lambda b, s: (b ^ 1, s)) for part in away]
    win = (3, 2, width, lanes)
    parts = []
    for e, other in enumerate(others):
        own, to_x, to_y, to_xy = call(
            functools.partial(project_kernel, dims, e),
            [(3, width, lanes)] * 4,
            (spreads, volumes, other),
            scratch=[VMEM((3, total, lanes), jnp.float32)],
        )
        from_xy = send(to_xy, lambda b, s: (b ^ 2, s ^ 1))
        from_x = send(to_x, lambda b, s: (b ^ 2, s))
        from_y = send(to_y, lambda b, s: (b, s ^ 1))
        parts += [own, from_x, from_y, from_xy]
    numbers = call(
        functools.partial(ready_kernel, bins), [(19, 8, 128)], (penalty, tv_weight, spreads)
    )[0]
    state = [(3, 10, width, lanes)] * 3 + [(3, 5, width, lanes), (9, 9, width, lanes)]
    f0, far, near, cross = call(
        functools.partial(sum_kernel, dims),
        [state[0], win, (3, 1, width, lanes), (3, 3, width, lanes)],
        (numbers, *parts),
    )
    far = send(far, lambda b, s: (b ^ 1, s + (2 if b % 2 else -2)))
    near = send(near, lambda b, s: (b, s + (-2 if b % 2 else 2)))
    cross = send(cross, lambda b, s: (b ^ 1, s))
    work = 150 * width * lanes
    scratch = [VMEM((3, width, lanes), jnp.float32)]
    inner = call(
        functools.partial(inner_kernel, dims),
        state + [(3, 3, width, lanes)],
        (numbers, cross, f0),
        None,
        scratch,
        {2: 0},
        12 * work,
    )
    blocks = call(
        functools.partial(outer_kernel, dims),
        state + [(3, rows, lanes)] * 4,
        (numbers, far, near, *inner),
        None,
        scratch,
        {3 + i: i for i in range(5)},
        9 * work,
    )[5:]

    def owner(t):
        def where(b, s):
            j = t ^ (2 * (b // 2) + s % 2) ^ twist_of(b % 2, s // 2, mesh_slab)
            z = (s // 2) * 8 + 4 * (b % 2) + j
            return z // mesh_slab, z % mesh_slab

        return where

    blocks = [send(block, owner(key)) for key, block in zip(ROUNDS, blocks)]
    out = [(3, 1, total, lanes)]
    early = call(
        functools.partial(gather_kernel, rows, ROUNDS[:3]),
        out,
        blocks[:3],
        scratch=[pltpu.SemaphoreType.DMA((3,))],
        out_space=pl.ANY,
    )
    return call(
        functools.partial(gather_kernel, rows, ROUNDS[3:]),
        out,
        (blocks[3], *early),
        [VMEM, pl.ANY],
        [pltpu.SemaphoreType.DMA((1,))],
        {1: 0},
        out_space=pl.ANY,
    )[0]


def solution(mesh):
    placed = (P("bin", "slab", None, None), P(), P(), P())
    return jax.shard_map(
        functools.partial(on_device, mesh.shape["bin"], mesh.shape["slab"]),
        mesh=mesh,
        in_specs=placed,
        out_specs=P(None, ("bin", "slab"), None, None),
        check_vma=False,
    )
```
